128 devices in a mesh: mesh: 128 (over y, z, x, core).
Axes of the slice: x: 4, y: 4, z: 4, core: 2. Of those that a mesh axis runs over, the one named last changes fastest.
Arguments:
- states: float32 [786432, 256], P('mesh'), may hold values from -30 to 30
- inv_sqrt_mass: float32 [786432], P('mesh'), may hold values from 0.25 to 1.75
- element_blocks: bfloat16 [2048, 512, 512], P('mesh'), may hold values from -0.25 to 0.25
- element_nodes: int32 [2048, 512], P('mesh'), may hold values from 0 to 6143, as said below
- element_counts: int32 [128], P('mesh'), may hold values from 1 to 16, as said below
- node_counts: int32 [128], replicated, may hold values from 4608 to 6144, as said below
- boundary_rows: int32 [128, 2, 384], P('mesh'), may hold values from 0 to 4607, as said below
Outputs:
- rotated: float32 [786432, 256], P('mesh')
The draws below stay inside these ranges and needn't reach their ends.
Inputs may be any that keep to these rules, and one draw needn't show every extreme that they name: `node_counts`: live node rows of each device; some device has 6144. `element_counts`: live element slots of each device (the first slots are live); some device has 16. `element_nodes`: every entry is below its device's node count. `boundary_rows`: for each device the 768 entries are distinct rows below 4608.
All inputs are finite; a program needn't handle non-finite values.
Results may differ from the reference program's by a relative error of at most 0.0077.
Values sent between devices are 32-bit elements; how exact they have to be, the bound alone decides.
No kernel may reach another device: no remote copies, remote signals or barrier semaphores. Data moves between devices by JAX's collectives and lax.ppermute only.
A program may use at most 128 MiB of HBM per device.

```python
import jax
import jax.numpy as jnp
from jax import lax

S = 256
NODE_EL = 512
CAP = 6144
ELEM_CAP = 16
LIVE_MIN = 4608
BND = 384
DEVICES = 128


def node_count_table(key):
    counts = jax.random.randint(jax.random.fold_in(key, 11), (DEVICES,), LIVE_MIN, CAP + 1)
    chosen = jax.random.randint(jax.random.fold_in(key, 12), (), 0, DEVICES)
    return counts.at[chosen].set(CAP).astype(jnp.int32)


def draw_node_counts(key, part):
    return node_count_table(key)


def draw_element_counts(key, part):
    lowest = max(1, ELEM_CAP // 8)
    base = jax.random.randint(jax.random.fold_in(key, 21), (DEVICES,), lowest, ELEM_CAP // 2 + 1)
    heavy = jax.random.randint(jax.random.fold_in(key, 22), (DEVICES,), 0, 8) == 0
    chosen = jax.random.randint(jax.random.fold_in(key, 23), (), 0, DEVICES)
    counts = jnp.where(heavy, ELEM_CAP, base)
    return counts.at[chosen].set(ELEM_CAP).astype(jnp.int32)


def draw_element_nodes(key, part):
    counts = node_count_table(key)
    picks = jax.random.randint(jax.random.fold_in(key, 31), (DEVICES, ELEM_CAP, NODE_EL), 0, counts[:, None, None])
    return picks.reshape(DEVICES * ELEM_CAP, NODE_EL).astype(jnp.int32)


def draw_boundary_rows(key, part):
    keys = jax.random.split(jax.random.fold_in(key, 41), DEVICES)
    picks = jax.vmap(lambda k: jax.random.permutation(k, LIVE_MIN)[:2 * BND])(keys)
    return picks.reshape(DEVICES, 2, BND).astype(jnp.int32)


def draw_states(key, part):
    device = (jnp.arange(DEVICES * CAP) // CAP).astype(jnp.float32)
    rise = (1.0 + 2.0 * device / (DEVICES - 1))[:, None]
    return rise * jnp.clip(jax.random.normal(jax.random.fold_in(key, 54), (DEVICES * CAP, S), jnp.float32), -6.0, 6.0)


def block_levels(own_key, dims, pieces, smallest, top_value):
    loudness = 1.0
    for axis_at, shards_of in pieces:
        draws = jax.random.uniform(jax.random.fold_in(jax.random.fold_in(own_key, 6), axis_at), (shards_of,), jnp.float32, smallest / len(pieces), top_value / len(pieces))
        loudness = loudness * jnp.repeat(jnp.exp(draws), dims[axis_at] // shards_of).reshape((-1,) + (1,) * (len(dims) - 1 - axis_at))
    return loudness


def noise(rng, extent, spread, limit, cuts=(), kind=jnp.bfloat16):
    drawn = jax.random.normal(rng, extent, jnp.float32) * spread
    if len(cuts) > 0:
        drawn = block_levels(rng, extent, cuts, -0.22, 0.18) * drawn
    return jnp.clip(drawn, min=-limit, max=limit).astype(kind)


def setup_inputs(seed: int = 0) -> dict:
    seeds = jax.random.split(jax.random.key(seed), 8)
    return {
        "states": draw_states(jax.random.fold_in(seeds[7], 71), 0),
        "inv_sqrt_mass": jnp.clip(1.0 + 0.15 * jax.random.normal(seeds[1], (DEVICES * CAP,), jnp.float32), 0.25, 1.75),
        "element_blocks": noise(seeds[2], (DEVICES * ELEM_CAP, NODE_EL, NODE_EL), NODE_EL ** -0.5, 0.25, ((0, 128),)),
        "element_nodes": draw_element_nodes(jax.random.fold_in(seeds[7], 71), 0),
        "element_counts": draw_element_counts(jax.random.fold_in(seeds[7], 71), 0),
        "node_counts": draw_node_counts(jax.random.fold_in(seeds[7], 71), 0),
        "boundary_rows": draw_boundary_rows(jax.random.fold_in(seeds[7], 71), 0),
    }


def take_rows(field, rows):
    return jax.vmap(lambda block, index: block[index])(field, rows)

def apply_ham(field, mass, blocks, nodes, ecounts, lower_rows, upper_rows):
    scaled = (mass[..., None] * field).astype(jnp.bfloat16)

    def per_device(items):
        values, mats, index, count = items

        def step(total, slot):
            rows = index[slot]
            part = jnp.dot(mats[slot].astype(jnp.float32), values[rows].astype(jnp.float32), preferred_element_type=jnp.float32)
            live = (slot < count).astype(jnp.float32)
            return (total.at[rows].add(part * live), None)
        total, _ = lax.scan(step, jnp.zeros((CAP, S), jnp.float32), jnp.arange(ELEM_CAP).astype(jnp.int32))
        return total
    local = lax.map(per_device, (scaled, blocks, nodes, ecounts))
    upper_vals = take_rows(local, upper_rows)
    lower_vals = take_rows(local, lower_rows)
    zero_rows = jnp.zeros((1, BND, S), jnp.float32)
    coming_up = jnp.concatenate([zero_rows, upper_vals[:-1]], axis=0)
    coming_down = jnp.concatenate([lower_vals[1:], zero_rows], axis=0)
    assembled = jax.vmap(lambda block, r1, a1, r2, a2: block.at[r1].add(a1).at[r2].add(a2))(local, lower_rows, coming_up, upper_rows, coming_down)
    return mass[..., None] * assembled

def reference(states, inv_sqrt_mass, element_blocks, element_nodes, element_counts, node_counts, boundary_rows):
    field = states.reshape(DEVICES, CAP, S)
    mass = inv_sqrt_mass.reshape(DEVICES, CAP)
    blocks = element_blocks.reshape(DEVICES, ELEM_CAP, NODE_EL, NODE_EL)
    nodes = element_nodes.reshape(DEVICES, ELEM_CAP, NODE_EL)
    lower_rows = boundary_rows[:, 0]
    upper_rows = boundary_rows[:, 1]
    src_field = jnp.concatenate([take_rows(field, lower_rows)[:1], take_rows(field, upper_rows)[:-1]], axis=0)
    src_mass = jnp.concatenate([take_rows(mass, lower_rows)[:1], take_rows(mass, upper_rows)[:-1]], axis=0)
    field = jax.vmap(lambda block, r, v: block.at[r].set(v))(field, lower_rows, src_field)
    mass = jax.vmap(lambda block, r, v: block.at[r].set(v))(mass, lower_rows, src_mass)
    center = 0.5
    half_width = 1.5

    def ham(v):
        return apply_ham(v, mass, blocks, nodes, element_counts, lower_rows, upper_rows)
    first = (ham(field) - center * field) / half_width
    second = 2.0 * (ham(first) - center * first) / half_width - field
    filtered = 2.0 * (ham(second) - center * second) / half_width - first
    row_index = jnp.arange(CAP).astype(jnp.int32)
    live = row_index[None, :] < node_counts[:, None]
    in_lower = jnp.any(row_index[None, :, None] == lower_rows[:, None, :], axis=2)
    device_index = jnp.arange(DEVICES).astype(jnp.int32)
    owned = live & jnp.logical_not(in_lower & (device_index[:, None] >= 1))
    weighted = jnp.where(owned[..., None], filtered, 0.0).reshape(DEVICES * CAP, S)
    total = (jnp.sum(node_counts) - BND * (DEVICES - 1)).astype(jnp.float32)
    gram = lax.dot_general(weighted.astype(jnp.float32), weighted.astype(jnp.float32), (((0,), (0,)), ((), ())), precision=lax.Precision.HIGHEST, preferred_element_type=jnp.float32) / total
    factor = jnp.linalg.cholesky(gram)
    inverse = jax.scipy.linalg.solve_triangular(factor, jnp.eye(S, dtype=jnp.float32), lower=True)
    flat = filtered.reshape(DEVICES * CAP, S)
    rotated = jnp.dot(flat.astype(jnp.float32), inverse.T.astype(jnp.float32), precision=lax.Precision.HIGHEST, preferred_element_type=jnp.float32)
    return jnp.where(live.reshape(DEVICES * CAP)[:, None], rotated, 0.0)
```

```python
import functools

import jax
import jax.numpy as jnp
from jax import lax
from jax.experimental import pallas as pl
from jax.experimental.pallas import tpu as pltpu
from jax.sharding import PartitionSpec as P

CENTER = 0.5
HALF_WIDTH = 1.5
LANES = 128
ACCS = 4
F32 = jnp.float32
SMEM = pl.BlockSpec(memory_space=pltpu.SMEM)
VMEM = pl.BlockSpec(memory_space=pltpu.VMEM)
HBM = pl.BlockSpec(memory_space=pl.ANY)


def passed_along(block, axis, distance):
    devices = range(lax.axis_size(axis))
    route = [(i - distance, i) for i in devices if i - distance in devices]
    return lax.ppermute(block, axis, route)


def pair(offset):
    return pl.ds(pl.multiple_of(offset, 2), 2)


def span(start, size):
    return pl.ds(pl.multiple_of(start, size), size)


def params(mib=60):
    return pltpu.CompilerParams(vmem_limit_bytes=mib * 2**20)


def mass_pick(rows, mass, out):
    shared = out.shape[0]

    def step(j, carry):
        out[j] = mass[rows[shared + j] // 2]
        return carry

    lax.fori_loop(0, shared, step, 0, unroll=8)


def split_rows(states, mass48, w_out, m_out):
    for i in range(states.shape[0] // LANES):
        m = jnp.broadcast_to(mass48[i : i + 1, :], (LANES, LANES)).T
        block = states[i * LANES : (i + 1) * LANES, :]
        for h in range(2):
            at = pl.ds(2 * i * LANES + h, LANES, stride=2)
            m_out[at, :] = m
            w_out[at, :] = m * block[:, h * LANES : (h + 1) * LANES]


def add_rows(target, rows, base, source):
    group = 8

    def step(g, carry):
        at = [rows[base + g * group + k] for k in range(group)]
        new = [target[pair(at[k]), :] + source[pair(2 * (g * group + k)), :] for k in range(group)]
        for k in range(group):
            target[pair(at[k]), :] = new[k]
        return carry

    lax.fori_loop(0, source.shape[0] // (2 * group), step, 0, unroll=2)


def take_rows(out, rows, base, source):
    def step(j, carry):
        out[pair(2 * j), :] = source[pair(rows[base + j]), :]
        return carry

    lax.fori_loop(0, out.shape[0] // 2, step, 0, unroll=16)


def ham_kernel(stage, *refs):
    it = iter(refs)
    info, nodes, rows = next(it), next(it), next(it)
    if stage == 1:
        mass_in, value_in = next(it), next(it)
    else:
        from_below, from_above = next(it), next(it)
    x_hbm, m_hbm = next(it), next(it)
    prev_hbm = next(it) if stage > 1 else None
    blocks_hbm = next(it)
    next_hbm, send_up, send_down = next(it), next(it), next(it)
    w_hbm = next(it) if stage < 3 else None
    m_out_hbm = next(it) if stage == 1 else None
    w, m = next(it), next(it)
    prev = next(it) if stage > 1 else None
    accs = [next(it) for _ in range(ACCS)]
    blocks, picked, parts = next(it), next(it), next(it)
    sems, block_sems = next(it), next(it)

    shared = send_up.shape[0] // 2
    size = picked.shape[0] // 2
    live = info[0]

    load_w = pltpu.make_async_copy(x_hbm, w, sems.at[0])
    load_m = pltpu.make_async_copy(m_hbm, m, sems.at[1])
    load_w.start()
    load_m.start()

    def block_copy(e):
        return pltpu.make_async_copy(blocks_hbm.at[e], blocks.at[e], block_sems.at[e])

    def start_block(e, carry):
        block_copy(e).start()
        return carry

    lax.fori_loop(0, live, start_block, 0)
    if stage > 1:
        load_prev = pltpu.make_async_copy(prev_hbm, prev, sems.at[2])
        load_prev.start()

    chunk = 512
    chunks = w.shape[0] // chunk

    def clear(c, carry):
        for acc in accs:
            acc[span(c * chunk, chunk), :] = jnp.zeros((chunk, LANES), F32)
        return carry

    lax.fori_loop(0, chunks, clear, 0)
    load_w.wait()
    if stage == 1:
        load_m.wait()

        @pl.when(info[2] > 0)
        def _():
            for h in range(2):
                picked[pl.ds(h, shared, stride=2), :] = value_in[:, h * LANES : (h + 1) * LANES]

            def step(j, carry):
                at = pair(rows[j])
                m_j = jnp.full((2, LANES), mass_in[j], F32)
                m[at, :] = m_j
                w[at, :] = m_j * picked[pair(2 * j), :]
                return carry

            lax.fori_loop(0, shared, step, 0, unroll=8)

        save_m = pltpu.make_async_copy(m, m_out_hbm, sems.at[1])
        save_m.start()
    else:
        add_rows(w, rows, 0, from_below)
        add_rows(w, rows, shared, from_above)
    if stage < 3:
        save_w = pltpu.make_async_copy(w, w_hbm, sems.at[0])
        save_w.start()

    def product(e):
        block_copy(e).wait()
        x = jnp.concatenate(
            [picked[pl.ds(h, size, stride=2), :].astype(jnp.bfloat16) for h in range(2)], axis=1
        )
        part = jnp.dot(blocks[e], x, preferred_element_type=F32)
        for h in range(2):
            parts[pl.ds(h, size, stride=2), :] = part[:, h * LANES : (h + 1) * LANES]

    def first_pick(j, carry):
        picked[pair(2 * j), :] = w[pair(nodes[j]), :]
        return carry

    lax.fori_loop(0, size, first_pick, 0, unroll=32)
    product(0)

    def element(e, carry):
        later = jnp.minimum(e + 1, live - 1)

        def move(g, inner):
            for k in range(ACCS):
                j = g * ACCS + k
                picked[pair(2 * j), :] = w[pair(nodes[later * size + j]), :]
                at = pair(nodes[e * size + j])
                accs[k][at, :] = accs[k][at, :] + parts[pair(2 * j), :]
            return inner

        lax.fori_loop(0, size // ACCS, move, 0, unroll=8)

        @pl.when(e + 1 < live)
        def _():
            product(later)

        return carry

    lax.fori_loop(0, live, element, 0)

    if stage > 1:
        load_m.wait()
        load_prev.wait()
    factor = 1.0 if stage == 1 else 2.0
    scale_h = factor / HALF_WIDTH
    scale_w = -factor * CENTER / HALF_WIDTH

    def combine(c, carry):
        at = span(c * chunk, chunk)
        total = accs[0][at, :]
        for acc in accs[1:]:
            total = total + acc[at, :]
        mass = m[at, :]
        total = scale_h * (mass * mass) * total
        accs[0][at, :] = total
        new = total + scale_w * w[at, :]
        if stage > 1:
            new = new - prev[at, :]
        accs[1][at, :] = new
        pltpu.make_async_copy(accs[1].at[at, :], next_hbm.at[at, :], sems.at[3]).start()
        return carry

    lax.fori_loop(0, chunks, combine, 0)
    take_rows(send_up, rows, shared, accs[0])
    take_rows(send_down, rows, 0, accs[0])
    pltpu.make_async_copy(accs[1], next_hbm, sems.at[3]).wait()
    if stage < 3:
        save_w.wait()
    if stage == 1:
        save_m.wait()


def ham(stage, operands, field, blocks, shared):
    tall = jax.ShapeDtypeStruct(field, F32)
    send = jax.ShapeDtypeStruct((2 * shared, LANES), F32)
    size = blocks.shape[1]
    n_out = 3 + (stage < 3) + (stage == 1)
    outs = [tall, send, send] + [tall] * (n_out - 3)
    out_specs = [HBM, VMEM, VMEM] + [HBM] * (n_out - 3)
    in_specs = [SMEM, SMEM, SMEM] + ([SMEM, VMEM] if stage == 1 else [VMEM, VMEM])
    in_specs += [HBM, HBM] + ([HBM] if stage > 1 else []) + [HBM]
    fields = [pltpu.VMEM(field, F32)] * (ACCS + 2 + (stage > 1))
    scratch = fields + [
        pltpu.VMEM(blocks.shape, blocks.dtype),
        pltpu.VMEM((2 * size, LANES), F32),
        pltpu.VMEM((2 * size, LANES), F32),
        pltpu.SemaphoreType.DMA((4,)),
        pltpu.SemaphoreType.DMA((blocks.shape[0],)),
    ]
    return pl.pallas_call(
        functools.partial(ham_kernel, stage),
        out_shape=outs,
        in_specs=in_specs,
        out_specs=out_specs,
        scratch_shapes=scratch,
        compiler_params=params(),
        name="ham%d" % stage,
    )(*operands)


def split3(x):
    high = x.astype(jnp.bfloat16)
    return high, (x - high.astype(F32)).astype(jnp.bfloat16)


def finish_kernel(info, rows, from_below, from_above, x_hbm, m_hbm, out, gram, w, m, sems):
    load_w = pltpu.make_async_copy(x_hbm, w, sems.at[0])
    load_m = pltpu.make_async_copy(m_hbm, m, sems.at[1])
    load_w.start()
    load_m.start()
    shared = from_below.shape[0] // 2
    load_w.wait()
    add_rows(w, rows, 0, from_below)
    add_rows(w, rows, shared, from_above)
    load_m.wait()
    n = 256
    chunks = out.shape[0] // n

    def divide(c, carry):
        for h in range(2):
            at = pl.ds(2 * n * c + h, n, stride=2)
            value = w[at, :] / m[at, :]
            out[span(c * n, n), h * LANES : (h + 1) * LANES] = value
            w[at, :] = value
        return carry

    lax.fori_loop(0, chunks, divide, 0)

    @pl.when(info[2] > 0)
    def _():
        def blank(j, carry):
            w[pair(rows[j]), :] = jnp.zeros((2, LANES), F32)
            return carry

        lax.fori_loop(0, shared, blank, 0, unroll=16)

    gram[...] = jnp.zeros_like(gram)
    limit = info[1]

    def add_chunk(c, carry):
        live = c * n + lax.broadcasted_iota(jnp.int32, (n, LANES), 0) < limit
        g = jnp.concatenate(
            [jnp.where(live, w[pl.ds(2 * n * c + h, n, stride=2), :], 0.0) for h in range(2)], axis=1
        )
        high, low = split3(g)
        dims = (((0,), (0,)), ((), ()))
        square = lax.dot_general(high, high, dims, preferred_element_type=F32)
        cross = lax.dot_general(high, low, dims, preferred_element_type=F32)
        gram[...] += square + (cross + cross.T)
        return carry

    lax.fori_loop(0, chunks, add_chunk, 0)


def body(
    states, inv_sqrt_mass, element_blocks, element_nodes, element_counts, node_counts, boundary_rows
):
    position = lax.axis_index("mesh")
    devices = lax.axis_size("mesh")
    row_total, width = states.shape
    shared = boundary_rows.shape[2]
    field = (2 * row_total, LANES)
    info = jnp.stack([element_counts[0], node_counts[position], position]).astype(jnp.int32)
    rows = 2 * boundary_rows.reshape(-1)
    nodes = 2 * element_nodes.reshape(-1)

    mass_send = pl.pallas_call(
        mass_pick,
        out_shape=jax.ShapeDtypeStruct((shared,), F32),
        in_specs=[SMEM, SMEM],
        out_specs=SMEM,
        name="mass_pick",
    )(rows, inv_sqrt_mass)
    owner_mass = passed_along(mass_send, "mesh", 1)
    owner_vals = passed_along(states[boundary_rows[0, 1]], "mesh", 1)
    tall = jax.ShapeDtypeStruct(field, F32)
    w0, m = pl.pallas_call(
        split_rows,
        out_shape=[tall, tall],
        in_specs=[VMEM, VMEM],
        out_specs=[VMEM, VMEM],
        compiler_params=params(),
        name="split_rows",
    )(states, inv_sqrt_mass.reshape(-1, LANES))

    w1, up, down, w0, m = ham(
        1,
        (info, nodes, rows, owner_mass, owner_vals, w0, m, element_blocks),
        field,
        element_blocks,
        shared,
    )
    up, down = passed_along(up, "mesh", 1), passed_along(down, "mesh", -1)
    w2, up, down, w1 = ham(
        2, (info, nodes, rows, up, down, w1, m, w0, element_blocks), field, element_blocks, shared
    )
    up, down = passed_along(up, "mesh", 1), passed_along(down, "mesh", -1)
    w3, up, down = ham(
        3, (info, nodes, rows, up, down, w2, m, w1, element_blocks), field, element_blocks, shared
    )
    up, down = passed_along(up, "mesh", 1), passed_along(down, "mesh", -1)
    filtered, gram = pl.pallas_call(
        finish_kernel,
        out_shape=[
            jax.ShapeDtypeStruct(states.shape, F32),
            jax.ShapeDtypeStruct((width, width), F32),
        ],
        in_specs=[SMEM, SMEM, VMEM, VMEM, HBM, HBM],
        out_specs=[VMEM, VMEM],
        scratch_shapes=[pltpu.VMEM(field, F32), pltpu.VMEM(field, F32), pltpu.SemaphoreType.DMA((2,))],
        compiler_params=params(),
        name="finish",
    )(info, rows, up, down, w3, m)

    gram = lax.psum(gram, "mesh")
    total = (jnp.sum(node_counts) - shared * (devices - 1)).astype(F32)
    gram = gram / total
    factor = jnp.linalg.cholesky(gram)
    inverse = jax.scipy.linalg.solve_triangular(factor, jnp.eye(width, dtype=F32), lower=True)
    rotated = jnp.dot(
        filtered, inverse.T, precision=lax.Precision.HIGHEST, preferred_element_type=F32
    )
    live = jnp.arange(row_total) < node_counts[position]
    return jnp.where(live[:, None], rotated, 0.0)


def solution(mesh):
    in_specs = (
        P("mesh", None),
        P("mesh"),
        P("mesh", None, None),
        P("mesh", None),
        P("mesh"),
        P(),
        P("mesh", None, None),
    )
    out_specs = P("mesh", None)
    return jax.shard_map(body, mesh=mesh, in_specs=in_specs, out_specs=out_specs, check_vma=False)
```

```python
import functools

import jax
import jax.numpy as jnp
from jax import lax
from jax.experimental import pallas as pl
from jax.experimental.pallas import tpu as pltpu
from jax.sharding import PartitionSpec as P

CENTER = 0.5
HALF_WIDTH = 1.5
LANES = 128
ACCS = 4
UNROLL = 64
F32 = jnp.float32
SMEM = pl.BlockSpec(memory_space=pltpu.SMEM)
VMEM = pl.BlockSpec(memory_space=pltpu.VMEM)
HBM = pl.BlockSpec(memory_space=pl.ANY)


def passed_along(block, axis, distance):
    devices = range(lax.axis_size(axis))
    route = [(i - distance, i) for i in devices if i - distance in devices]
    return lax.ppermute(block, axis, route)


def pair(offset):
    return pl.ds(pl.multiple_of(offset, 2), 2)


def span(start, size):
    return pl.ds(pl.multiple_of(start, size), size)


def params(mib=60):
    return pltpu.CompilerParams(vmem_limit_bytes=mib * 2**20)


def send_rows(rows, mass, states_hbm, values_out, mass_out, left, right, sems):
    sides = (left, right)
    loads = [
        pltpu.make_async_copy(states_hbm.at[:, h * LANES : (h + 1) * LANES], sides[h], sems.at[h])
        for h in range(2)
    ]
    for load in loads:
        load.start()
    shared = mass_out.shape[0]
    unroll = 16

    def mass_step(g, carry):
        some = rows.at[pl.ds(shared + g * unroll, unroll)]
        for k in range(unroll):
            mass_out[g * unroll + k] = mass[some[k] // 2]
        return carry

    lax.fori_loop(0, shared // unroll, mass_step, 0)
    for load in loads:
        load.wait()

    def step(g, carry):
        some = rows.at[pl.ds(shared + g * unroll, unroll)]
        base = pl.multiple_of(2 * g * unroll, 2 * unroll)
        for k in range(unroll):
            row = some[k] // 2
            for h in range(2):
                values_out[pl.ds(base + 2 * k + h, 1), :] = sides[h][pl.ds(row, 1), :]
        return carry

    lax.fori_loop(0, shared // unroll, step, 0)


def split_rows(mass_all, states, w_out, m_out):
    step = pl.program_id(0)
    per = states.shape[0] // LANES
    for i in range(per):
        m = jnp.broadcast_to(mass_all[pl.ds(step * per + i, 1), :], (LANES, LANES)).T
        block = states[i * LANES : (i + 1) * LANES, :]
        for h in range(2):
            at = pl.ds(2 * i * LANES + h, LANES, stride=2)
            m_out[at, :] = m
            w_out[at, :] = m * block[:, h * LANES : (h + 1) * LANES]


def add_rows(target, rows, base, source):
    group = 16

    def step(g, carry):
        some = rows.at[pl.ds(base + g * group, group)]
        first = pl.multiple_of(2 * g * group, 2 * group)
        at = [pair(some[k]) for k in range(group)]
        new = [target[at[k], :] + source[pl.ds(first + 2 * k, 2), :] for k in range(group)]
        for k in range(group):
            target[at[k], :] = new[k]
        return carry

    lax.fori_loop(0, source.shape[0] // (2 * group), step, 0)


def take_rows(out, rows, base, source):
    group = 32

    def step(g, carry):
        some = rows.at[pl.ds(base + g * group, group)]
        first = pl.multiple_of(2 * g * group, 2 * group)
        for k in range(group):
            out[pl.ds(first + 2 * k, 2), :] = source[pair(some[k]), :]
        return carry

    lax.fori_loop(0, out.shape[0] // (2 * group), step, 0)


def ham_kernel(stage, *refs):
    it = iter(refs)
    count, position, nodes, rows = next(it), next(it), next(it), next(it)
    if stage == 1:
        mass_in, value_in = next(it), next(it)
    else:
        from_below, from_above = next(it), next(it)
    x_hbm, m_hbm = next(it), next(it)
    prev_hbm = next(it) if stage > 1 else None
    blocks_hbm = next(it)
    next_hbm, send_up, send_down = next(it), next(it), next(it)
    w_hbm = next(it) if stage < 3 else None
    m_out_hbm = next(it) if stage == 1 else None
    w, m = next(it), next(it)
    prev = next(it) if stage > 1 else None
    accs = [next(it) for _ in range(ACCS)]
    blocks, picked, parts = next(it), next(it), next(it)
    sems, block_sems = next(it), next(it)

    shared = send_up.shape[0] // 2
    size = picked.shape[0] // 2
    live = count[0]

    load_w = pltpu.make_async_copy(x_hbm, w, sems.at[0])
    load_m = pltpu.make_async_copy(m_hbm, m, sems.at[1])
    load_w.start()
    if stage == 1:
        load_m.start()

    def block_copy(e):
        return pltpu.make_async_copy(blocks_hbm.at[e], blocks.at[e], block_sems.at[e])

    def start_block(e, carry):
        block_copy(e).start()
        return carry

    block_copy(0).start()
    chunk = 512
    chunks = w.shape[0] // chunk

    def clear(c, carry):
        for acc in accs:
            acc[span(c * chunk, chunk), :] = jnp.zeros((chunk, LANES), F32)
        return carry

    lax.fori_loop(0, chunks, clear, 0)
    load_w.wait()
    lax.fori_loop(1, live, start_block, 0)
    if stage == 1:
        load_m.wait()

        @pl.when(position[0] > 0)
        def _():
            def step(j, carry):
                at = pair(rows[j])
                m_j = jnp.full((2, LANES), mass_in[j], F32)
                m[at, :] = m_j
                w[at, :] = m_j * value_in[pair(2 * j), :]
                return carry

            lax.fori_loop(0, shared, step, 0, unroll=8)

        save_m = pltpu.make_async_copy(m, m_out_hbm, sems.at[1])
        save_m.start()
    else:
        load_m.start()
        load_prev = pltpu.make_async_copy(prev_hbm, prev, sems.at[2])
        load_prev.start()
        add_rows(w, rows, 0, from_below)
        add_rows(w, rows, shared, from_above)
    if stage < 3:
        save_w = pltpu.make_async_copy(w, w_hbm, sems.at[0])
        save_w.start()

    def product(e):
        block_copy(e).wait()
        x = jnp.concatenate(
            [picked[pl.ds(h, size, stride=2), :].astype(jnp.bfloat16) for h in range(2)], axis=1
        )
        part = jnp.dot(blocks[e], x, preferred_element_type=F32)
        for h in range(2):
            parts[pl.ds(h, size, stride=2), :] = part[:, h * LANES : (h + 1) * LANES]

    take_rows(picked, nodes, 0, w)
    product(0)

    def element(e, carry):
        later = jnp.minimum(e + 1, live - 1)

        def move(g, inner):
            here = nodes.at[pl.ds(e * size + g * UNROLL, UNROLL)]
            ahead = nodes.at[pl.ds(later * size + g * UNROLL, UNROLL)]
            first = pl.multiple_of(2 * g * UNROLL, 2 * UNROLL)
            for k in range(UNROLL):
                line = pl.ds(first + 2 * k, 2)
                picked[line, :] = w[pair(ahead[k]), :]
                at = pair(here[k])
                acc = accs[k % ACCS]
                acc[at, :] = acc[at, :] + parts[line, :]
            return inner

        lax.fori_loop(0, size // UNROLL, move, 0)

        @pl.when(e + 1 < live)
        def _():
            product(later)

        return carry

    lax.fori_loop(0, live, element, 0)

    if stage > 1:
        load_m.wait()
        load_prev.wait()
    factor = 1.0 if stage == 1 else 2.0
    scale_h = factor / HALF_WIDTH
    scale_w = -factor * CENTER / HALF_WIDTH

    def combine(c, carry):
        at = span(c * chunk, chunk)
        total = accs[0][at, :]
        for acc in accs[1:]:
            total = total + acc[at, :]
        mass = m[at, :]
        rest = scale_w * w[at, :]
        if stage > 1:
            rest = rest - prev[at, :]
        if stage < 3:
            total = scale_h * (mass * mass) * total
        else:
            total = scale_h * mass * total
            rest = rest / mass
        accs[0][at, :] = total
        accs[1][at, :] = total + rest
        pltpu.make_async_copy(accs[1].at[at, :], next_hbm.at[at, :], sems.at[3]).start()
        return carry

    lax.fori_loop(0, chunks, combine, 0)
    take_rows(send_up, rows, shared, accs[0])
    take_rows(send_down, rows, 0, accs[0])
    pltpu.make_async_copy(accs[1], next_hbm, sems.at[3]).wait()
    if stage < 3:
        save_w.wait()
    if stage == 1:
        save_m.wait()


def ham(stage, operands, field, blocks, shared):
    tall = jax.ShapeDtypeStruct(field, F32)
    send = jax.ShapeDtypeStruct((2 * shared, LANES), F32)
    size = blocks.shape[1]
    n_out = 3 + (stage < 3) + (stage == 1)
    outs = [tall, send, send] + [tall] * (n_out - 3)
    out_specs = [HBM, VMEM, VMEM] + [HBM] * (n_out - 3)
    in_specs = [SMEM, SMEM, SMEM, SMEM] + ([SMEM, VMEM] if stage == 1 else [VMEM, VMEM])
    in_specs += [HBM, HBM] + ([HBM] if stage > 1 else []) + [HBM]
    fields = [pltpu.VMEM(field, F32)] * (ACCS + 2 + (stage > 1))
    scratch = fields + [
        pltpu.VMEM(blocks.shape, blocks.dtype),
        pltpu.VMEM((2 * size, LANES), F32),
        pltpu.VMEM((2 * size, LANES), F32),
        pltpu.SemaphoreType.DMA((4,)),
        pltpu.SemaphoreType.DMA((blocks.shape[0],)),
    ]
    return pl.pallas_call(
        functools.partial(ham_kernel, stage),
        out_shape=outs,
        in_specs=in_specs,
        out_specs=out_specs,
        scratch_shapes=scratch,
        compiler_params=params(),
        name="ham%d" % stage,
    )(*operands)


def high_low(x):
    high = x.astype(jnp.bfloat16)
    return high, (x - high.astype(F32)).astype(jnp.bfloat16)


def halves(ref, start, size):
    return jnp.concatenate([ref[pl.ds(start + h, size, stride=2), :] for h in range(2)], axis=1)


def finish_kernel(
    counts, position, rows, from_below, from_above, x_hbm, f_hbm, keep, give, w, shared_rows, gram, sems
):
    load = pltpu.make_async_copy(x_hbm, w, sems.at[0])
    load.start()
    shared = from_below.shape[0] // 2
    width = 2 * LANES
    gram[...] = jnp.zeros_like(gram)
    load.wait()
    add_rows(w, rows, 0, from_below)
    add_rows(w, rows, shared, from_above)
    save = pltpu.make_async_copy(w, f_hbm, sems.at[1])
    save.start()
    take_rows(shared_rows, rows, 0, w)
    limit = counts[position[0]]
    n = 256
    dims = (((0,), (0,)), ((), ()))

    def add_chunk(c, carry):
        live = c * n + lax.broadcasted_iota(jnp.int32, (n, width), 0) < limit
        high, low = high_low(jnp.where(live, halves(w, 2 * n * c, n), 0.0))
        gram[...] += lax.dot_general(
            high, jnp.concatenate([high, low], axis=1), dims, preferred_element_type=F32
        )
        return carry

    lax.fori_loop(0, pl.cdiv(limit, n), add_chunk, 0)

    @pl.when(position[0] > 0)
    def _():
        high, low = high_low(halves(shared_rows, 0, shared))
        gram[...] -= lax.dot_general(
            high, jnp.concatenate([high, low], axis=1), dims, preferred_element_type=F32
        )

    cross = gram[:, width:]
    full = gram[:, :width] + (cross + cross.T)
    row = lax.broadcasted_iota(jnp.int32, (LANES, LANES), 0)
    lane = lax.broadcasted_iota(jnp.int32, (LANES, LANES), 1)
    last = full[LANES:, LANES:]
    both = jnp.where(row >= lane, full[:LANES, :LANES], last)
    diagonal = jnp.sum(jnp.where(row == lane, last, 0.0), axis=0, keepdims=True)
    pieces = (
        (both, jnp.broadcast_to(diagonal, (8, LANES))),
        (full[:LANES, LANES:], jnp.zeros((8, LANES), F32)),
    )
    for core in range(2):

        @pl.when(position[0] % 2 == core)
        def _():
            for out, (block, tail) in ((keep, pieces[core]), (give, pieces[1 - core])):
                out[0:LANES, :] = block
                out[LANES : LANES + 8, :] = tail

    save.wait()


def shifted(value, stride, radix, by):
    route = []
    for i in range(lax.axis_size("mesh")):
        digit = i // stride % radix
        route.append((i, i + ((digit + by) % radix - digit) * stride))
    return lax.ppermute(value, "mesh", route)


def sum_over_devices(keep, give):
    total = keep + shifted(give, 1, 2, 1)
    stride, devices = 2, lax.axis_size("mesh")
    while stride < devices:
        radix = min(4, devices // stride)
        got = [shifted(total, stride, radix, by) for by in range(1, radix)]
        for piece in got:
            total = total + piece
        stride *= radix
    return total, shifted(total, 1, 2, 1)


def eliminate(block):
    n = block.shape[0]
    lane = lax.broadcasted_iota(jnp.int32, (8, n), 1)
    sub = lax.broadcasted_iota(jnp.int32, (8, n), 0)
    parts = [block[8 * i : 8 * i + 8, :] for i in range(n // 8)]
    for k in range(n):
        q, s = divmod(k, 8)
        row = parts[q][s : s + 1, :]
        rec = 1.0 / jnp.broadcast_to(row[:, k : k + 1], (1, n))
        row = jnp.broadcast_to(jnp.where(lane[:1] == k, 1.0, row) * rec, (8, n))
        for i in range(q, n // 8):
            col = jnp.broadcast_to(parts[i][:, k : k + 1], (8, n))
            new = jnp.where(lane == k, 0.0, parts[i]) - col * row
            parts[i] = jnp.where(sub > s, new, parts[i]) if i == q else new
    done = []
    for i in range(n // 8):
        here = sub + 8 * i
        pivot = jnp.sum(jnp.where(lane == here, parts[i], 0.0), axis=1, keepdims=True)
        unit = jnp.where(lane < here, parts[i], jnp.where(lane == here, 1.0, 0.0))
        done.append(unit * lax.rsqrt(pivot))
    return jnp.concatenate(done, axis=0)


def dot32(a, b, ca, cb):
    return lax.dot_general(
        a,
        b,
        (((ca,), (cb,)), ((), ())),
        precision=lax.Precision.HIGHEST,
        preferred_element_type=F32,
    )


def rotate_kernel(
    counts, position, mine, other, f_hbm, out_hbm, w, out, block, factors, basis, sems, *, total_of
):
    load = pltpu.make_async_copy(f_hbm, w, sems.at[0])
    load.start()
    total = lax.fori_loop(0, counts.shape[0], lambda i, t: t + counts[i], jnp.int32(0))
    scale = 1.0 / (jnp.full((LANES, LANES), total_of(total), jnp.int32).astype(F32))
    core = jnp.full((LANES + 8, LANES), position[0] % 2, jnp.int32)
    first = jnp.where(core == 0, mine[...], other[...])
    second = jnp.where(core == 0, other[...], mine[...])
    row = lax.broadcasted_iota(jnp.int32, (LANES, LANES), 0)
    lane = lax.broadcasted_iota(jnp.int32, (LANES, LANES), 1)
    both = first[:LANES, :]
    turned = both.T
    block[...] = jnp.where(row >= lane, both, turned) * scale
    right = second[:LANES, :] * scale
    last = jnp.where(row < lane, both, turned)
    last = jnp.where(row == lane, jnp.broadcast_to(first[LANES : LANES + 1, :], (LANES, LANES)), last)
    factors[2] = last * scale

    def panel(p, carry):
        factors[p] = eliminate(block[...])

        @pl.when(p == 0)
        def _():
            side = dot32(factors[0], right, 1, 0)
            block[...] = factors[2] - dot32(side, side, 0, 0)
            factors[2] = side

        return carry

    lax.fori_loop(0, 2, panel, 0)
    n = 2 * LANES
    top = factors[0].T
    low_right = factors[1].T
    corner = -dot32(top, dot32(factors[2], low_right, 1, 0), 1, 0)
    inverse_t = jnp.concatenate(
        [
            jnp.concatenate([top, corner], axis=1),
            jnp.concatenate([jnp.zeros((LANES, LANES), F32), low_right], axis=1),
        ],
        axis=0,
    )
    basis[0:n, :], basis[n : 2 * n, :] = high_low(inverse_t)
    limit = counts[position[0]]
    load.wait()
    size = 512

    def chunk(c, carry):
        at = span(c * size, size)
        high, low = high_low(halves(w, 2 * size * c, size))
        value = jnp.dot(high, basis[0:n, :], preferred_element_type=F32)
        value += jnp.dot(high, basis[n : 2 * n, :], preferred_element_type=F32)
        value += jnp.dot(low, basis[0:n, :], preferred_element_type=F32)
        live = c * size + lax.broadcasted_iota(jnp.int32, (size, n), 0) < limit
        out[at, :] = jnp.where(live, value, 0.0)
        pltpu.make_async_copy(out.at[at, :], out_hbm.at[at, :], sems.at[1]).start()
        return carry

    lax.fori_loop(0, out.shape[0] // size, chunk, 0)
    pltpu.make_async_copy(out, out_hbm, sems.at[1]).wait()


def body(
    states, inv_sqrt_mass, element_blocks, element_nodes, element_counts, node_counts, boundary_rows
):
    position = lax.axis_index("mesh").astype(jnp.int32).reshape(1)
    devices = lax.axis_size("mesh")
    row_total, width = states.shape
    shared = boundary_rows.shape[2]
    field = (2 * row_total, LANES)
    rows = 2 * boundary_rows.reshape(-1)
    nodes = 2 * element_nodes.reshape(-1)
    tall = jax.ShapeDtypeStruct(field, F32)
    send = jax.ShapeDtypeStruct((2 * shared, LANES), F32)

    values, masses = pl.pallas_call(
        send_rows,
        out_shape=[send, jax.ShapeDtypeStruct((shared,), F32)],
        in_specs=[SMEM, SMEM, HBM],
        out_specs=[VMEM, SMEM],
        scratch_shapes=[
            pltpu.VMEM((row_total, LANES), F32),
            pltpu.VMEM((row_total, LANES), F32),
            pltpu.SemaphoreType.DMA((2,)),
        ],
        compiler_params=params(),
        name="send_rows",
    )(rows, inv_sqrt_mass, states)
    owner_mass = passed_along(masses, "mesh", 1)
    owner_vals = passed_along(values, "mesh", 1)
    step = 1024
    w0, m = pl.pallas_call(
        split_rows,
        grid=(row_total // step,),
        out_shape=[tall, tall],
        in_specs=[VMEM, pl.BlockSpec((step, width), lambda i: (i, 0))],
        out_specs=[pl.BlockSpec((2 * step, LANES), lambda i: (i, 0))] * 2,
        compiler_params=params(),
        cost_estimate=pl.CostEstimate(
            flops=row_total * width, bytes_accessed=12 * row_total * width, transcendentals=0
        ),
        name="split_rows",
    )(inv_sqrt_mass.reshape(-1, LANES), states)

    head = (element_counts, position, nodes, rows)
    args = (field, element_blocks, shared)
    w1, up, down, w0, m = ham(1, head + (owner_mass, owner_vals, w0, m, element_blocks), *args)
    up, down = passed_along(up, "mesh", 1), passed_along(down, "mesh", -1)
    w2, up, down, w1 = ham(2, head + (up, down, w1, m, w0, element_blocks), *args)
    up, down = passed_along(up, "mesh", 1), passed_along(down, "mesh", -1)
    w3, up, down = ham(3, head + (up, down, w2, m, w1, element_blocks), *args)
    up, down = passed_along(up, "mesh", 1), passed_along(down, "mesh", -1)
    half = jax.ShapeDtypeStruct((LANES + 8, LANES), F32)
    filtered, keep, give = pl.pallas_call(
        finish_kernel,
        out_shape=[tall, half, half],
        in_specs=[SMEM, SMEM, SMEM, VMEM, VMEM, HBM],
        out_specs=[HBM, VMEM, VMEM],
        scratch_shapes=[
            pltpu.VMEM(field, F32),
            pltpu.VMEM((2 * shared, LANES), F32),
            pltpu.VMEM((width, 2 * width), F32),
            pltpu.SemaphoreType.DMA((2,)),
        ],
        compiler_params=params(),
        name="finish",
    )(node_counts, position, rows, up, down, w3)

    mine, other = sum_over_devices(keep, give)
    return pl.pallas_call(
        functools.partial(rotate_kernel, total_of=lambda t: t - shared * (devices - 1)),
        out_shape=jax.ShapeDtypeStruct(states.shape, F32),
        in_specs=[SMEM, SMEM, VMEM, VMEM, HBM],
        out_specs=HBM,
        scratch_shapes=[
            pltpu.VMEM(field, F32),
            pltpu.VMEM(states.shape, F32),
            pltpu.VMEM((LANES, LANES), F32),
            pltpu.VMEM((3, LANES, LANES), F32),
            pltpu.VMEM((2 * width, width), jnp.bfloat16),
            pltpu.SemaphoreType.DMA((2,)),
        ],
        compiler_params=params(),
        name="rotate",
    )(node_counts, position, mine, other, filtered)


def solution(mesh):
    in_specs = (
        P("mesh", None),
        P("mesh"),
        P("mesh", None, None),
        P("mesh", None),
        P("mesh"),
        P(),
        P("mesh", None, None),
    )
    out_specs = P("mesh", None)
    return jax.shard_map(body, mesh=mesh, in_specs=in_specs, out_specs=out_specs, check_vma=False)
```

```python
import functools

import jax
import jax.numpy as jnp
from jax import lax
from jax.experimental import pallas as pl
from jax.experimental.pallas import tpu as pltpu
from jax.sharding import PartitionSpec as P

CENTER = 0.5
HALF_WIDTH = 1.5
LANES = 128
ACCS = 4
UNROLL = 64
F32 = jnp.float32
SMEM = pl.BlockSpec(memory_space=pltpu.SMEM)
VMEM = pl.BlockSpec(memory_space=pltpu.VMEM)
HBM = pl.BlockSpec(memory_space=pl.ANY)
KEPT = object()


def passed_along(block, axis, distance):
    devices = range(lax.axis_size(axis))
    route = [(i - distance, i) for i in devices if i - distance in devices]
    return lax.ppermute(block, axis, route)


def pair(offset):
    return pl.ds(pl.multiple_of(offset, 2), 2)


def span(start, size):
    return pl.ds(pl.multiple_of(start, size), size)


def call(name, kernel, ins, outs, aliases=None, scratch=(), mib=8, flops=0):
    operands, in_specs = [], []
    for value, spec in ins:
        if spec is KEPT:
            value = pltpu.with_memory_space_constraint(value, pltpu.VMEM)
        elif spec is HBM:
            value = pltpu.with_memory_space_constraint(value, pltpu.HBM)
        operands.append(value)
        in_specs.append(VMEM if spec is KEPT else spec)
    return pl.pallas_call(
        kernel,
        out_shape=[
            pltpu.VMEM(shape, dtype) if spec is KEPT else jax.ShapeDtypeStruct(shape, dtype)
            for (shape, dtype), spec in outs
        ],
        in_specs=in_specs,
        out_specs=[VMEM if spec is KEPT else spec for _, spec in outs],
        input_output_aliases=aliases or {},
        scratch_shapes=list(scratch),
        compiler_params=pltpu.CompilerParams(vmem_limit_bytes=mib * 2**20),
        cost_estimate=pl.CostEstimate(flops=flops, bytes_accessed=flops, transcendentals=0),
        name=name,
    )(*operands)


def start_kernel(position, rows, mass_all, states_hbm, w, m, send, stage, picked, sems):
    count = mass_all.shape[0]
    total = count * LANES
    group = 8
    parts = count // group

    def load(part, h):
        at = span(part * group * LANES, group * LANES)
        return pltpu.make_async_copy(
            states_hbm.at[at, h * LANES : (h + 1) * LANES], stage.at[h, at, :], sems.at[part, h]
        )

    for part in range(parts):
        for h in range(2):
            load(part, h).start()
    for part in range(parts):
        for h in range(2):
            load(part, h).wait()

        def convert(i, carry):
            at = part * group + i
            mass = jnp.broadcast_to(mass_all[pl.ds(at, 1), :], (LANES, LANES)).T
            base = 2 * LANES * at
            for h in range(2):
                m[pl.ds(base + h, LANES, stride=2), :] = mass
                w[pl.ds(base + h, LANES, stride=2), :] = mass * stage[h, span(LANES * at, LANES), :]
            return carry

        lax.fori_loop(0, group, convert, 0)
    shared = picked.shape[0]
    take_rows(send.at[0 : 2 * shared, :], rows, shared, w)
    unroll = 32

    def pick(g, carry):
        some = rows.at[pl.ds(shared + g * unroll, unroll)]
        for k in range(unroll):
            picked[pl.ds(g * unroll + k, 1), :] = m[pl.ds(some[k], 1), :]
        return carry

    lax.fori_loop(0, shared // unroll, pick, 0)
    diagonal = lax.broadcasted_iota(jnp.int32, (LANES, LANES), 0) == lax.broadcasted_iota(
        jnp.int32, (LANES, LANES), 1
    )
    send[2 * shared : 2 * shared + 8, :] = jnp.zeros((8, LANES), F32)
    for i in range(shared // LANES):
        block = picked[i * LANES : (i + 1) * LANES, :]
        line = jnp.sum(jnp.where(diagonal, block, 0.0), axis=0, keepdims=True)
        send[2 * shared + i : 2 * shared + i + 1, :] = line


def clear_kernel(after, *accs):
    chunk = 512

    def clear(c, carry):
        for acc in accs:
            acc[span(c * chunk, chunk), :] = jnp.zeros((chunk, LANES), F32)
        return carry

    lax.fori_loop(0, accs[0].shape[0] // chunk, clear, 0)


def take_rows(out, rows, base, *sources):
    group = 32

    def step(g, carry):
        some = rows.at[pl.ds(base + g * group, group)]
        first = pl.multiple_of(2 * g * group, 2 * group)
        for k in range(group):
            at = pair(some[k])
            total = sources[0][at, :]
            for source in sources[1:]:
                total = total + source[at, :]
            out[pl.ds(first + 2 * k, 2), :] = total
        return carry

    lax.fori_loop(0, out.shape[0] // (2 * group), step, 0)


def add_rows(target, rows, base, source, m, scale):
    group = 16

    def step(g, carry):
        some = rows.at[pl.ds(base + g * group, group)]
        first = pl.multiple_of(2 * g * group, 2 * group)
        at = [pair(some[k]) for k in range(group)]
        new = []
        for k in range(group):
            mass = m[at[k], :]
            new.append(target[at[k], :] + scale * (mass * mass) * source[pl.ds(first + 2 * k, 2), :])
        for k in range(group):
            target[at[k], :] = new[k]
        return carry

    lax.fori_loop(0, source.shape[0] // (2 * group), step, 0)


def near_base(position, shared):
    return jnp.where(position % 2 == 0, shared, 0)


def ham_kernel(stage, *refs):
    count, position, nodes, rows = refs[:4]
    n_in = 1 if stage == 1 else 2
    received = refs[4 : 4 + n_in]
    refs = refs[4 + n_in :]
    n_field = 2 + ACCS
    blocks_hbm = refs[n_field]
    refs = refs[n_field + 1 :]
    w, m, *accs = refs[:n_field]
    send_near, send_far, picked, parts, lines, blocks, sems = refs[n_field:]

    shared = send_near.shape[0] // 2
    size = picked.shape[0] // 2
    live = count[0]
    near = near_base(position[0], shared)
    far = shared - near

    def load(e):
        return pltpu.make_async_copy(blocks_hbm.at[e], blocks.at[e % 2], sems.at[e % 2])

    load(0).start()

    if stage == 1:
        (owner,) = received

        @pl.when(position[0] > 0)
        def _():
            for i in range(shared // LANES):
                line = owner[2 * shared + i : 2 * shared + i + 1, :]
                lines[i * LANES : (i + 1) * LANES, :] = jnp.broadcast_to(line, (LANES, LANES)).T
            unroll = 16

            def patch(g, carry):
                some = rows.at[pl.ds(g * unroll, unroll)]
                first = pl.multiple_of(g * unroll, unroll)
                for k in range(unroll):
                    at = pair(some[k])
                    w[at, :] = owner[pl.ds(2 * first + 2 * k, 2), :]
                    m[at, :] = jnp.broadcast_to(lines[pl.ds(first + k, 1), :], (2, LANES))
                return carry

            lax.fori_loop(0, shared // unroll, patch, 0)
    else:
        scale = (1.0 if stage == 2 else 2.0) / HALF_WIDTH
        add_rows(w, rows, near, received[0], m, scale)
        add_rows(w, rows, far, received[1], m, scale)

    def product(e):
        load(e).wait()

        @pl.when(e + 1 < live)
        def _():
            load(e + 1).start()

        x = jnp.concatenate(
            [picked[pl.ds(h, size, stride=2), :].astype(jnp.bfloat16) for h in range(2)], axis=1
        )
        part = jnp.dot(blocks[e % 2], x, preferred_element_type=F32)
        for h in range(2):
            parts[pl.ds(h, size, stride=2), :] = part[:, h * LANES : (h + 1) * LANES]

    take_rows(picked, nodes, 0, w)
    product(0)

    def element(e, carry):
        later = jnp.minimum(e + 1, live - 1)

        def move(g, inner):
            here = nodes.at[pl.ds(e * size + g * UNROLL, UNROLL)]
            ahead = nodes.at[pl.ds(later * size + g * UNROLL, UNROLL)]
            first = pl.multiple_of(2 * g * UNROLL, 2 * UNROLL)
            for k in range(UNROLL):
                line = pl.ds(first + 2 * k, 2)
                picked[line, :] = w[pair(ahead[k]), :]
                at = pair(here[k])
                acc = accs[k % ACCS]
                acc[at, :] = acc[at, :] + parts[line, :]
            return inner

        lax.fori_loop(0, size // UNROLL, move, 0)

        @pl.when(e + 1 < live)
        def _():
            product(later)

        return carry

    lax.fori_loop(0, live, element, 0)
    take_rows(send_near, rows, near, *accs)
    take_rows(send_far, rows, far, *accs)


def combine_kernel(stage, *refs):
    n = 2 + ACCS + (stage > 1)
    w, m = refs[:2]
    accs = refs[n - ACCS : n]
    old = refs[2] if stage > 1 else None
    new, *emptied = refs[n:]
    factor = 1.0 if stage == 1 else 2.0
    scale_h = factor / HALF_WIDTH
    scale_w = -factor * CENTER / HALF_WIDTH
    chunk = 256

    def step(c, carry):
        at = span(c * chunk, chunk)
        total = accs[0][at, :]
        for acc in accs[1:]:
            total = total + acc[at, :]
        mass = m[at, :]
        rest = scale_w * w[at, :]
        if stage > 1:
            rest = rest - old[at, :]
        if stage < 3:
            new[at, :] = scale_h * (mass * mass) * total + rest
        else:
            new[at, :] = scale_h * mass * total + rest / mass
        for acc in emptied:
            acc[at, :] = jnp.zeros((chunk, LANES), F32)
        return carry

    lax.fori_loop(0, w.shape[0] // chunk, step, 0)


def high_low(x):
    high = x.astype(jnp.bfloat16)
    return high, (x - high.astype(F32)).astype(jnp.bfloat16)


def halves(ref, start, size):
    return jnp.concatenate([ref[pl.ds(start + h, size, stride=2), :] for h in range(2)], axis=1)


def add_square(gram, value, size):
    high, low = high_low(value)
    gram[...] += lax.dot_general(
        high,
        jnp.concatenate([high, low], axis=1),
        (((0,), (0,)), ((), ())),
        preferred_element_type=F32,
    )


def inner_kernel(counts, position, rows, f_in, f, saved, gram):
    shared = saved.shape[0] // 4
    take_rows(saved, rows, 0, f)
    unroll = 32

    def blank(g, carry):
        some = rows.at[pl.ds(g * unroll, unroll)]
        for k in range(unroll):
            f[pair(some[k]), :] = jnp.zeros((2, LANES), F32)
        return carry

    lax.fori_loop(0, 2 * shared // unroll, blank, 0)
    gram[...] = jnp.zeros_like(gram)
    limit = counts[position[0]]
    n = 256

    def add_chunk(c, carry):
        live = c * n + lax.broadcasted_iota(jnp.int32, (n, 2 * LANES), 0) < limit
        add_square(gram, jnp.where(live, halves(f, 2 * n * c, n), 0.0), n)
        return carry

    lax.fori_loop(0, pl.cdiv(limit, n), add_chunk, 0)


def finish_kernel(
    position, rows, near_in, far_in, m, saved_in, gram_in, f_in, f, keep, give, saved, gram
):
    shared = near_in.shape[0] // 2
    width = 2 * LANES
    near = near_base(position[0], shared)
    far = shared - near
    scale = 2.0 / HALF_WIDTH
    group = 16

    def step(g, carry):
        for base, source in ((near, near_in), (far, far_in)):
            some = rows.at[pl.ds(base + g * group, group)]
            first = pl.multiple_of(2 * g * group, 2 * group)
            for k in range(group):
                at = pair(some[k])
                line = pair(2 * base + first + 2 * k)
                value = saved_in[line, :] + scale * m[at, :] * source[pl.ds(first + 2 * k, 2), :]
                saved[line, :] = value
                f[at, :] = value
        return carry

    lax.fori_loop(0, shared // group, step, 0)
    gram[...] = gram_in[...]
    add_square(gram, halves(saved, 2 * shared, shared), shared)

    @pl.when(position[0] == 0)
    def _():
        add_square(gram, halves(saved, 0, shared), shared)

    cross = gram[:, width:]
    full = gram[:, :width] + (cross + cross.T)
    row = lax.broadcasted_iota(jnp.int32, (LANES, LANES), 0)
    lane = lax.broadcasted_iota(jnp.int32, (LANES, LANES), 1)
    last = full[LANES:, LANES:]
    both = jnp.where(row >= lane, full[:LANES, :LANES], last)
    diagonal = jnp.sum(jnp.where(row == lane, last, 0.0), axis=0, keepdims=True)
    pieces = (
        (both, jnp.broadcast_to(diagonal, (8, LANES))),
        (full[:LANES, LANES:], jnp.zeros((8, LANES), F32)),
    )
    for core in range(2):

        @pl.when(position[0] % 2 == core)
        def _():
            for out, (block, tail) in ((keep, pieces[core]), (give, pieces[1 - core])):
                out[0:LANES, :] = block
                out[LANES : LANES + 8, :] = tail


def shifted(value, stride, radix, by):
    route = []
    for i in range(lax.axis_size("mesh")):
        digit = i // stride % radix
        route.append((i, i + ((digit + by) % radix - digit) * stride))
    return lax.ppermute(value, "mesh", route)


def add_kernel(*refs):
    total = refs[0][...]
    for ref in refs[1:-1]:
        total = total + ref[...]
    refs[-1][...] = total


def added(*values):
    ins = [(value, VMEM) for value in values]
    return call("add", add_kernel, ins, [((values[0].shape, F32), VMEM)], mib=1)[0]


def sum_over_devices(keep, give):
    total = added(keep, shifted(give, 1, 2, 1))
    stride, devices = 2, lax.axis_size("mesh")
    while stride < devices:
        radix = min(4, devices // stride)
        got = [shifted(total, stride, radix, by) for by in range(1, radix)]
        total = added(total, *got)
        stride *= radix
    return total, shifted(total, 1, 2, 1)


def eliminate(block):
    n = block.shape[0]
    lane = lax.broadcasted_iota(jnp.int32, (8, n), 1)
    sub = lax.broadcasted_iota(jnp.int32, (8, n), 0)
    parts = [block[8 * i : 8 * i + 8, :] for i in range(n // 8)]
    for k in range(n):
        q, s = divmod(k, 8)
        row = parts[q][s : s + 1, :]
        rec = 1.0 / jnp.broadcast_to(row[:, k : k + 1], (1, n))
        row = jnp.broadcast_to(jnp.where(lane[:1] == k, 1.0, row) * rec, (8, n))
        for i in range(q, n // 8):
            col = jnp.broadcast_to(parts[i][:, k : k + 1], (8, n))
            new = jnp.where(lane == k, 0.0, parts[i]) - col * row
            parts[i] = jnp.where(sub > s, new, parts[i]) if i == q else new
    done = []
    for i in range(n // 8):
        here = sub + 8 * i
        pivot = jnp.sum(jnp.where(lane == here, parts[i], 0.0), axis=1, keepdims=True)
        unit = jnp.where(lane < here, parts[i], jnp.where(lane == here, 1.0, 0.0))
        done.append(unit * lax.rsqrt(pivot))
    return jnp.concatenate(done, axis=0)


def dot32(a, b, ca, cb):
    return lax.dot_general(
        a,
        b,
        (((ca,), (cb,)), ((), ())),
        precision=lax.Precision.HIGHEST,
        preferred_element_type=F32,
    )


def rotate_kernel(
    counts, position, mine, other, w, out_hbm, out, block, factors, basis, sems, *, total_of
):
    total = lax.fori_loop(0, counts.shape[0], lambda i, t: t + counts[i], jnp.int32(0))
    scale = 1.0 / (jnp.full((LANES, LANES), total_of(total), jnp.int32).astype(F32))
    core = jnp.full((LANES + 8, LANES), position[0] % 2, jnp.int32)
    first = jnp.where(core == 0, mine[...], other[...])
    second = jnp.where(core == 0, other[...], mine[...])
    row = lax.broadcasted_iota(jnp.int32, (LANES, LANES), 0)
    lane = lax.broadcasted_iota(jnp.int32, (LANES, LANES), 1)
    both = first[:LANES, :]
    turned = both.T
    block[...] = jnp.where(row >= lane, both, turned) * scale
    right = second[:LANES, :] * scale
    last = jnp.where(row < lane, both, turned)
    last = jnp.where(row == lane, jnp.broadcast_to(first[LANES : LANES + 1, :], (LANES, LANES)), last)
    factors[2] = last * scale

    def panel(p, carry):
        factors[p] = eliminate(block[...])

        @pl.when(p == 0)
        def _():
            side = dot32(factors[0], right, 1, 0)
            block[...] = factors[2] - dot32(side, side, 0, 0)
            factors[2] = side

        return carry

    lax.fori_loop(0, 2, panel, 0)
    n = 2 * LANES
    top = factors[0].T
    low_right = factors[1].T
    corner = -dot32(top, dot32(factors[2], low_right, 1, 0), 1, 0)
    inverse_t = jnp.concatenate(
        [
            jnp.concatenate([top, corner], axis=1),
            jnp.concatenate([jnp.zeros((LANES, LANES), F32), low_right], axis=1),
        ],
        axis=0,
    )
    basis[0:n, :], basis[n : 2 * n, :] = high_low(inverse_t)
    limit = counts[position[0]]
    size = 512

    def chunk(c, carry):
        at = span(c * size, size)
        high, low = high_low(halves(w, 2 * size * c, size))
        value = jnp.dot(high, basis[0:n, :], preferred_element_type=F32)
        value += jnp.dot(high, basis[n : 2 * n, :], preferred_element_type=F32)
        value += jnp.dot(low, basis[0:n, :], preferred_element_type=F32)
        live = c * size + lax.broadcasted_iota(jnp.int32, (size, n), 0) < limit
        out[at, :] = jnp.where(live, value, 0.0)
        pltpu.make_async_copy(out.at[at, :], out_hbm.at[at, :], sems.at[0]).start()
        return carry

    lax.fori_loop(0, out.shape[0] // size, chunk, 0)
    pltpu.make_async_copy(out, out_hbm, sems.at[0]).wait()


def exchanged(near, far):
    n = lax.axis_size("mesh")
    far = lax.ppermute(far, "mesh", [(i, i - 1 + 2 * (i % 2)) for i in range(1, n - 1)])
    near = lax.ppermute(near, "mesh", [(i, i ^ 1) for i in range(n)])
    return near, far


def body(
    states, inv_sqrt_mass, element_blocks, element_nodes, element_counts, node_counts, boundary_rows
):
    position = lax.axis_index("mesh").astype(jnp.int32).reshape(1)
    devices = lax.axis_size("mesh")
    row_total, width = states.shape
    shared = boundary_rows.shape[2]
    size = element_blocks.shape[1]
    rows = 2 * boundary_rows.reshape(-1)
    nodes = 2 * element_nodes.reshape(-1)
    tall = ((2 * row_total, LANES), F32)
    send = ((2 * shared, LANES), F32)
    mass_rows = inv_sqrt_mass.reshape(-1, LANES)

    w0, m, values = call(
        "start",
        start_kernel,
        [(position, SMEM), (rows, SMEM), (mass_rows, VMEM), (states, HBM)],
        [(tall, KEPT), (tall, KEPT), (((2 * shared + 8, LANES), F32), VMEM)],
        scratch=[
            pltpu.VMEM((2, row_total, LANES), F32),
            pltpu.VMEM((shared, LANES), F32),
            pltpu.SemaphoreType.DMA((mass_rows.shape[0] // 8, 2)),
        ],
        mib=12,
    )
    owner = passed_along(values, "mesh", 1)
    accs = call(
        "clear",
        clear_kernel,
        [(w0, KEPT)],
        [(tall, KEPT)] * ACCS,
        mib=1,
        flops=10 * row_total * width,
    )

    def ham(stage, received, w, m, accs):
        ins = [(element_counts, SMEM), (position, SMEM), (nodes, SMEM), (rows, SMEM)]
        ins += [(r, VMEM) for r in received]
        first = len(ins)
        ins += [(v, KEPT) for v in (w, m, *accs)] + [(element_blocks, HBM)]
        w, m, *accs, near, far = call(
            "ham%d" % stage,
            functools.partial(ham_kernel, stage),
            ins,
            [(tall, KEPT)] * (2 + ACCS) + [(send, VMEM)] * 2,
            aliases={first + i: i for i in range(2 + ACCS)},
            scratch=[
                pltpu.VMEM((2 * size, LANES), F32),
                pltpu.VMEM((2 * size, LANES), F32),
                pltpu.VMEM((shared, LANES), F32),
                pltpu.VMEM((2, *element_blocks.shape[1:]), element_blocks.dtype),
                pltpu.SemaphoreType.DMA((2,)),
            ],
            mib=4,
        )
        return w, m, accs, near, far

    def combine(stage, w, m, old, accs):
        ins = [(w, KEPT), (m, KEPT)] + ([(old, KEPT)] if stage > 1 else [])
        first = len(ins)
        ins += [(acc, KEPT) for acc in accs]
        aliases = {first + i: 1 + i for i in range(ACCS)}
        if stage > 1:
            aliases[2] = 0
        new, *accs = call(
            "combine%d" % stage,
            functools.partial(combine_kernel, stage),
            ins,
            [(tall, KEPT)] * (1 + ACCS),
            aliases=aliases,
            mib=1,
            flops=10 * row_total * width,
        )
        return new, accs

    w0, m, accs, near, far = ham(1, [owner], w0, m, accs)
    received = exchanged(near, far)
    w1, accs = combine(1, w0, m, None, accs)
    w1, m, accs, near, far = ham(2, received, w1, m, accs)
    received = exchanged(near, far)
    w2, accs = combine(2, w1, m, w0, accs)
    w2, m, accs, near, far = ham(3, received, w2, m, accs)
    received = exchanged(near, far)
    f, accs = combine(3, w2, m, w1, accs)
    wide = ((width, 2 * width), F32)
    pool = ((4 * shared, LANES), F32)
    f, saved, gram = call(
        "inner",
        inner_kernel,
        [(node_counts, SMEM), (position, SMEM), (rows, SMEM), (f, KEPT)],
        [(tall, KEPT), (pool, KEPT), (wide, KEPT)],
        aliases={3: 0},
        mib=4,
        flops=10 * row_total * width,
    )
    half = ((LANES + 8, LANES), F32)
    f, keep, give = call(
        "finish",
        finish_kernel,
        [(position, SMEM), (rows, SMEM), (received[0], VMEM), (received[1], VMEM)]
        + [(m, KEPT), (saved, KEPT), (gram, KEPT), (f, KEPT)],
        [(tall, KEPT), (half, VMEM), (half, VMEM)],
        aliases={7: 0},
        scratch=[pltpu.VMEM(*pool), pltpu.VMEM(*wide)],
        mib=4,
    )
    mine, other = sum_over_devices(keep, give)
    (rotated,) = call(
        "rotate",
        functools.partial(rotate_kernel, total_of=lambda t: t - shared * (devices - 1)),
        [(node_counts, SMEM), (position, SMEM), (mine, VMEM), (other, VMEM), (f, KEPT)],
        [((states.shape, F32), HBM)],
        scratch=[
            pltpu.VMEM(states.shape, F32),
            pltpu.VMEM((LANES, LANES), F32),
            pltpu.VMEM((3, LANES, LANES), F32),
            pltpu.VMEM((2 * width, width), jnp.bfloat16),
            pltpu.SemaphoreType.DMA((1,)),
        ],
        mib=24,
    )
    return rotated


def solution(mesh):
    in_specs = (
        P("mesh", None),
        P("mesh"),
        P("mesh", None, None),
        P("mesh", None),
        P("mesh"),
        P(),
        P("mesh", None, None),
    )
    out_specs = P("mesh", None)
    return jax.shard_map(body, mesh=mesh, in_specs=in_specs, out_specs=out_specs, check_vma=False)
```

```python
import functools

import jax
import jax.numpy as jnp
from jax import lax
from jax.experimental import pallas as pl
from jax.experimental.pallas import tpu as pltpu
from jax.sharding import PartitionSpec as P

CENTER = 0.5
HALF_WIDTH = 1.5
LANES = 128
ACCS = 4
UNROLL = 256
F32 = jnp.float32
SMEM = pl.BlockSpec(memory_space=pltpu.SMEM)
VMEM = pl.BlockSpec(memory_space=pltpu.VMEM)
HBM = pl.BlockSpec(memory_space=pl.ANY)
KEPT = object()


def passed_along(block, axis, distance):
    devices = range(lax.axis_size(axis))
    route = [(i - distance, i) for i in devices if i - distance in devices]
    return lax.ppermute(block, axis, route)


def pair(offset):
    return pl.ds(pl.multiple_of(offset, 2), 2)


def span(start, size):
    return pl.ds(pl.multiple_of(start, size), size)


def call(name, kernel, ins, outs, aliases=None, scratch=(), mib=8, flops=0):
    operands, in_specs = [], []
    for value, spec in ins:
        if spec is KEPT:
            value = pltpu.with_memory_space_constraint(value, pltpu.VMEM)
        elif spec is HBM:
            value = pltpu.with_memory_space_constraint(value, pltpu.HBM)
        operands.append(value)
        in_specs.append(VMEM if spec is KEPT else spec)
    return pl.pallas_call(
        kernel,
        out_shape=[
            pltpu.VMEM(shape, dtype) if spec is KEPT else jax.ShapeDtypeStruct(shape, dtype)
            for (shape, dtype), spec in outs
        ],
        in_specs=in_specs,
        out_specs=[VMEM if spec is KEPT else spec for _, spec in outs],
        input_output_aliases=aliases or {},
        scratch_shapes=list(scratch),
        compiler_params=pltpu.CompilerParams(vmem_limit_bytes=mib * 2**20),
        cost_estimate=pl.CostEstimate(flops=flops, bytes_accessed=flops, transcendentals=0),
        name=name,
    )(*operands)


def start_kernel(position, rows, mass, states_hbm, stage, send, lines, sems):
    shared = lines.shape[0]
    total = mass.shape[0]
    loads = [
        pltpu.make_async_copy(
            states_hbm.at[:, h * LANES : (h + 1) * LANES],
            stage.at[h * total : (h + 1) * total, :],
            sems.at[h],
        )
        for h in range(2)
    ]
    for load in loads:
        load.start()
    unroll = 32

    def spread(g, carry):
        some = rows.at[pl.ds(shared + g * unroll, unroll)]
        for k in range(unroll):
            lines[pl.ds(g * unroll + k, 1), :] = jnp.full((1, LANES), mass[some[k] // 2], F32)
        return carry

    lax.fori_loop(0, shared // unroll, spread, 0)
    diagonal = lax.broadcasted_iota(jnp.int32, (LANES, LANES), 0) == lax.broadcasted_iota(
        jnp.int32, (LANES, LANES), 1
    )
    send[2 * shared : 2 * shared + 8, :] = jnp.zeros((8, LANES), F32)
    for i in range(shared // LANES):
        block = lines[i * LANES : (i + 1) * LANES, :]
        line = jnp.sum(jnp.where(diagonal, block, 0.0), axis=0, keepdims=True)
        send[2 * shared + i : 2 * shared + i + 1, :] = line
    for load in loads:
        load.wait()

    def pick(g, carry):
        some = rows.at[pl.ds(shared + g * unroll, unroll)]
        first = pl.multiple_of(g * unroll, unroll)
        for k in range(unroll):
            row = some[k] // 2
            line = lines[pl.ds(first + k, 1), :]
            for h in range(2):
                value = stage[pl.ds(h * total + row, 1), :]
                send[pl.ds(2 * first + 2 * k + h, 1), :] = line * value
        return carry

    lax.fori_loop(0, shared // unroll, pick, 0)


def convert_kernel(mass_all, stage, w, m, *accs):
    count = mass_all.shape[0]
    total = count * LANES

    def convert(i, carry):
        mass = jnp.broadcast_to(mass_all[pl.ds(i, 1), :], (LANES, LANES)).T
        base = 2 * LANES * i
        for h in range(2):
            m[pl.ds(base + h, LANES, stride=2), :] = mass
            w[pl.ds(base + h, LANES, stride=2), :] = mass * stage[span(h * total + LANES * i, LANES), :]
        for acc in accs[:-1]:
            acc[span(base, 2 * LANES), :] = jnp.zeros((2 * LANES, LANES), F32)
        return carry

    lax.fori_loop(0, count, convert, 0)

    def clear(i, carry):
        accs[-1][span(2 * LANES * i, 2 * LANES), :] = jnp.zeros((2 * LANES, LANES), F32)
        return carry

    lax.fori_loop(0, count, clear, 0)


def take_rows(out, rows, base, *sources):
    group = 32

    def step(g, carry):
        some = rows.at[pl.ds(base + g * group, group)]
        first = pl.multiple_of(2 * g * group, 2 * group)
        for k in range(group):
            at = pair(some[k])
            total = sources[0][at, :]
            for source in sources[1:]:
                total = total + source[at, :]
            out[pl.ds(first + 2 * k, 2), :] = total
        return carry

    lax.fori_loop(0, out.shape[0] // (2 * group), step, 0)


def add_rows(target, rows, base, source, m, scale):
    group = 16

    def step(g, carry):
        some = rows.at[pl.ds(base + g * group, group)]
        first = pl.multiple_of(2 * g * group, 2 * group)
        at = [pair(some[k]) for k in range(group)]
        new = []
        for k in range(group):
            mass = m[at[k], :]
            new.append(target[at[k], :] + scale * (mass * mass) * source[pl.ds(first + 2 * k, 2), :])
        for k in range(group):
            target[at[k], :] = new[k]
        return carry

    lax.fori_loop(0, source.shape[0] // (2 * group), step, 0)


def near_base(position, shared):
    return jnp.where(position % 2 == 0, shared, 0)


def ham_kernel(stage, *refs):
    count, position, nodes, rows = refs[:4]
    n_in = 1 if stage == 1 else 2
    received = refs[4 : 4 + n_in]
    refs = refs[4 + n_in :]
    n_field = 2 + ACCS
    blocks_hbm = refs[n_field]
    refs = refs[n_field + 1 :]
    w, m, *accs = refs[:n_field]
    send_near, send_far, picked, x, *parts_pair, lines, block_a, block_b, sems = refs[n_field:]
    block_pair = (block_a, block_b)

    shared = send_near.shape[0] // 2
    size = picked.shape[0] // 2
    live = count[0]
    near = near_base(position[0], shared)
    far = shared - near

    def load(e, parity):
        return pltpu.make_async_copy(blocks_hbm.at[e], block_pair[parity], sems.at[parity])

    load(0, 0).start()

    @pl.when(live > 1)
    def _():
        load(1, 1).start()

    if stage == 1:
        (owner,) = received

        @pl.when(position[0] > 0)
        def _():
            for i in range(shared // LANES):
                line = owner[2 * shared + i : 2 * shared + i + 1, :]
                lines[i * LANES : (i + 1) * LANES, :] = jnp.broadcast_to(line, (LANES, LANES)).T
            unroll = 16

            def patch(g, carry):
                some = rows.at[pl.ds(g * unroll, unroll)]
                first = pl.multiple_of(g * unroll, unroll)
                for k in range(unroll):
                    at = pair(some[k])
                    w[at, :] = owner[pl.ds(2 * first + 2 * k, 2), :]
                    m[at, :] = jnp.broadcast_to(lines[pl.ds(first + k, 1), :], (2, LANES))
                return carry

            lax.fori_loop(0, shared // unroll, patch, 0)
    else:
        scale = (1.0 if stage == 2 else 2.0) / HALF_WIDTH
        add_rows(w, rows, near, received[0], m, scale)
        add_rows(w, rows, far, received[1], m, scale)

    def convert():
        for h in range(2):
            x[:, h * LANES : (h + 1) * LANES] = picked[pl.ds(h, size, stride=2), :].astype(x.dtype)

    def product(parity, g):
        part = jnp.dot(
            block_pair[parity][span(g * UNROLL, UNROLL), :], x[...], preferred_element_type=F32
        )
        for h in range(2):
            at = pl.ds(2 * UNROLL * g + h, UNROLL, stride=2)
            parts_pair[parity][at, :] = part[:, h * LANES : (h + 1) * LANES]

    take_rows(picked, nodes, 0, w)
    convert()
    load(0, 0).wait()

    def first_product(g, carry):
        product(0, g)
        return carry

    lax.fori_loop(0, size // UNROLL, first_product, 0)
    take_rows(picked, nodes, jnp.minimum(1, live - 1) * size, w)
    convert()

    def element(e, parity):
        other = 1 - parity
        last = live - 1

        @pl.when(e + 2 < live)
        def _():
            load(e + 2, parity).start()

        @pl.when(e + 1 < live)
        def _():
            load(e + 1, other).wait()

        def move(g, inner):
            product(other, g)
            here = nodes.at[pl.ds(e * size + g * UNROLL, UNROLL)]
            ahead = nodes.at[pl.ds(jnp.minimum(e + 2, last) * size + g * UNROLL, UNROLL)]
            first = pl.multiple_of(2 * g * UNROLL, 2 * UNROLL)
            for k in range(UNROLL):
                line = pl.ds(first + 2 * k, 2)
                picked[line, :] = w[pair(ahead[k]), :]
                at = pair(here[k])
                acc = accs[k % ACCS]
                acc[at, :] = acc[at, :] + parts_pair[parity][line, :]
            return inner

        lax.fori_loop(0, size // UNROLL, move, 0)
        convert()

    def two(t, carry):
        element(2 * t, 0)

        @pl.when(2 * t + 1 < live)
        def _():
            element(2 * t + 1, 1)

        return carry

    lax.fori_loop(0, pl.cdiv(live, 2), two, 0)
    take_rows(send_near, rows, near, *accs)
    take_rows(send_far, rows, far, *accs)


def combine_kernel(stage, *refs):
    n = 2 + ACCS + (stage > 1)
    w, m = refs[:2]
    accs = refs[n - ACCS : n]
    old = refs[2] if stage > 1 else None
    new, *emptied = refs[n:]
    factor = 1.0 if stage == 1 else 2.0
    scale_h = factor / HALF_WIDTH
    scale_w = -factor * CENTER / HALF_WIDTH
    chunk = 64

    def step(c, carry):
        at = span(c * chunk, chunk)
        total = accs[0][at, :]
        for acc in accs[1:]:
            total = total + acc[at, :]
        mass = m[at, :]
        rest = scale_w * w[at, :]
        if stage > 1:
            rest = rest - old[at, :]
        if stage < 3:
            new[at, :] = scale_h * (mass * mass) * total + rest
        else:
            new[at, :] = scale_h * mass * total + rest / mass
        for acc in emptied:
            acc[at, :] = jnp.zeros((chunk, LANES), F32)
        return carry

    lax.fori_loop(0, w.shape[0] // chunk, step, 0)


def high_low(x):
    high = x.astype(jnp.bfloat16)
    return high, (x - high.astype(F32)).astype(jnp.bfloat16)


def halves(ref, start, size):
    return jnp.concatenate([ref[pl.ds(start + h, size, stride=2), :] for h in range(2)], axis=1)


def add_square(gram, value, size):
    high, low = high_low(value)
    gram[...] += lax.dot_general(
        high,
        jnp.concatenate([high, low], axis=1),
        (((0,), (0,)), ((), ())),
        preferred_element_type=F32,
    )


def inner_kernel(counts, position, rows, f_in, f, saved, gram):
    shared = saved.shape[0] // 4
    take_rows(saved, rows, 0, f)
    unroll = 32

    def blank(g, carry):
        some = rows.at[pl.ds(g * unroll, unroll)]
        for k in range(unroll):
            f[pair(some[k]), :] = jnp.zeros((2, LANES), F32)
        return carry

    lax.fori_loop(0, 2 * shared // unroll, blank, 0)
    gram[...] = jnp.zeros_like(gram)
    limit = counts[position[0]]
    n = 512

    def add_chunk(c, carry):
        live = c * n + lax.broadcasted_iota(jnp.int32, (n, 2 * LANES), 0) < limit
        add_square(gram, jnp.where(live, halves(f, 2 * n * c, n), 0.0), n)
        return carry

    lax.fori_loop(0, pl.cdiv(limit, n), add_chunk, 0)


def finish_kernel(
    position, rows, near_in, far_in, m, saved_in, gram_in, f_in, f, keep, give, saved, gram
):
    shared = near_in.shape[0] // 2
    width = 2 * LANES
    near = near_base(position[0], shared)
    far = shared - near
    scale = 2.0 / HALF_WIDTH
    group = 16

    def step(g, carry):
        for base, source in ((near, near_in), (far, far_in)):
            some = rows.at[pl.ds(base + g * group, group)]
            first = pl.multiple_of(2 * g * group, 2 * group)
            for k in range(group):
                at = pair(some[k])
                line = pair(2 * base + first + 2 * k)
                value = saved_in[line, :] + scale * m[at, :] * source[pl.ds(first + 2 * k, 2), :]
                saved[line, :] = value
                f[at, :] = value
        return carry

    lax.fori_loop(0, shared // group, step, 0)
    gram[...] = gram_in[...]
    add_square(gram, halves(saved, 2 * shared, shared), shared)

    @pl.when(position[0] == 0)
    def _():
        add_square(gram, halves(saved, 0, shared), shared)

    cross = gram[:, width:]
    full = gram[:, :width] + (cross + cross.T)
    row = lax.broadcasted_iota(jnp.int32, (LANES, LANES), 0)
    lane = lax.broadcasted_iota(jnp.int32, (LANES, LANES), 1)
    last = full[LANES:, LANES:]
    both = jnp.where(row >= lane, full[:LANES, :LANES], last)
    diagonal = jnp.sum(jnp.where(row == lane, last, 0.0), axis=0, keepdims=True)
    pieces = (
        (both, jnp.broadcast_to(diagonal, (8, LANES))),
        (full[:LANES, LANES:], jnp.zeros((8, LANES), F32)),
    )
    for core in range(2):

        @pl.when(position[0] % 2 == core)
        def _():
            for out, (block, tail) in ((keep, pieces[core]), (give, pieces[1 - core])):
                out[0:LANES, :] = block
                out[LANES : LANES + 8, :] = tail


def shifted(value, stride, radix, by):
    route = []
    for i in range(lax.axis_size("mesh")):
        digit = i // stride % radix
        route.append((i, i + ((digit + by) % radix - digit) * stride))
    return lax.ppermute(value, "mesh", route)


def add_kernel(*refs):
    total = refs[0][...]
    for ref in refs[1:-1]:
        total = total + ref[...]
    refs[-1][...] = total


def added(*values):
    ins = [(value, VMEM) for value in values]
    return call("add", add_kernel, ins, [((values[0].shape, F32), VMEM)], mib=1)[0]


def sum_over_devices(keep, give):
    total = added(keep, shifted(give, 1, 2, 1))
    stride, devices = 2, lax.axis_size("mesh")
    while stride < devices:
        radix = min(4, devices // stride)
        got = [shifted(total, stride, radix, by) for by in range(1, radix)]
        total = added(total, *got)
        stride *= radix
    return total, shifted(total, 1, 2, 1)


def eliminate(block):
    n = block.shape[0]
    b = 8
    lane = lax.broadcasted_iota(jnp.int32, (b, n), 1)
    sub = lax.broadcasted_iota(jnp.int32, (b, n), 0)

    def line(value, s):
        return jnp.broadcast_to(value[s : s + 1, :], (b, n))

    def columns(value, first):
        return [jnp.broadcast_to(value[:, first + c : first + c + 1], (b, n)) for c in range(b)]

    parts = [block[b * i : b * i + b, :] for i in range(n // b)]
    for q in range(n // b):
        first = b * q
        inside = (lane >= first) & (lane < first + b)
        cols = columns(parts[q], first)
        corner = [[line(cols[c], s) for c in range(s + 1)] for s in range(b)]
        own = jnp.where(inside, jnp.where(lane - first == sub, 1.0, 0.0), parts[q])
        rows = [line(own, s) for s in range(b)]
        recs, low = [], [[None] * b for _ in range(b)]
        for c in range(b):
            recs.append(1.0 / corner[c][c])
            for s in range(c + 1, b):
                low[s][c] = corner[s][c] * recs[c]
            for s in range(c + 1, b):
                for t in range(c + 1, s + 1):
                    corner[s][t] = corner[s][t] - low[s][c] * corner[t][c]
                rows[s] = rows[s] - low[s][c] * rows[c]
        done = jnp.zeros((b, n), F32)
        for s in range(b):
            done = jnp.where(sub == s, rows[s] * lax.rsqrt(corner[s][s]), done)
        solved = [rows[s] * recs[s] for s in range(b)]
        for s in reversed(range(b)):
            for c in range(s):
                solved[c] = solved[c] - low[s][c] * solved[s]
        for i in range(q + 1, n // b):
            cols = columns(parts[i], first)
            terms = [cols[c] * solved[c] for c in range(b)]
            while len(terms) > 1:
                terms = [terms[k] + terms[k + 1] for k in range(0, len(terms), 2)]
            parts[i] = jnp.where(inside, 0.0, parts[i]) - terms[0]
        parts[q] = jnp.where(lane < first + b, done, 0.0)
    return jnp.concatenate(parts, axis=0)


def dot32(a, b, ca, cb):
    return lax.dot_general(
        a,
        b,
        (((ca,), (cb,)), ((), ())),
        precision=lax.Precision.HIGHEST,
        preferred_element_type=F32,
    )


def rotate_kernel(
    counts, position, mine, other, w, out_hbm, out, block, factors, basis, sems, *, total_of
):
    total = lax.fori_loop(0, counts.shape[0], lambda i, t: t + counts[i], jnp.int32(0))
    scale = 1.0 / (jnp.full((LANES, LANES), total_of(total), jnp.int32).astype(F32))
    core = jnp.full((LANES + 8, LANES), position[0] % 2, jnp.int32)
    first = jnp.where(core == 0, mine[...], other[...])
    second = jnp.where(core == 0, other[...], mine[...])
    row = lax.broadcasted_iota(jnp.int32, (LANES, LANES), 0)
    lane = lax.broadcasted_iota(jnp.int32, (LANES, LANES), 1)
    both = first[:LANES, :]
    turned = both.T
    block[...] = jnp.where(row >= lane, both, turned) * scale
    right = second[:LANES, :] * scale
    last = jnp.where(row < lane, both, turned)
    last = jnp.where(row == lane, jnp.broadcast_to(first[LANES : LANES + 1, :], (LANES, LANES)), last)
    factors[2] = last * scale

    def panel(p, carry):
        factors[p] = eliminate(block[...])

        @pl.when(p == 0)
        def _():
            side = dot32(factors[0], right, 1, 0)
            block[...] = factors[2] - dot32(side, side, 0, 0)
            factors[2] = side

        return carry

    lax.fori_loop(0, 2, panel, 0)
    n = 2 * LANES
    top = factors[0].T
    low_right = factors[1].T
    corner = -dot32(top, dot32(factors[2], low_right, 1, 0), 1, 0)
    inverse_t = jnp.concatenate(
        [
            jnp.concatenate([top, corner], axis=1),
            jnp.concatenate([jnp.zeros((LANES, LANES), F32), low_right], axis=1),
        ],
        axis=0,
    )
    basis[0:n, :], basis[n : 2 * n, :] = high_low(inverse_t)
    limit = counts[position[0]]
    size = 512

    def chunk(c, carry):
        at = span(c * size, size)
        high, low = high_low(halves(w, 2 * size * c, size))
        value = jnp.dot(high, basis[0:n, :], preferred_element_type=F32)
        value += jnp.dot(high, basis[n : 2 * n, :], preferred_element_type=F32)
        value += jnp.dot(low, basis[0:n, :], preferred_element_type=F32)
        live = c * size + lax.broadcasted_iota(jnp.int32, (size, n), 0) < limit
        out[at, :] = jnp.where(live, value, 0.0)
        pltpu.make_async_copy(out.at[at, :], out_hbm.at[at, :], sems.at[0]).start()
        return carry

    lax.fori_loop(0, out.shape[0] // size, chunk, 0)
    pltpu.make_async_copy(out, out_hbm, sems.at[0]).wait()


def exchanged(near, far):
    n = lax.axis_size("mesh")
    far = lax.ppermute(far, "mesh", [(i, i - 1 + 2 * (i % 2)) for i in range(1, n - 1)])
    near = lax.ppermute(near, "mesh", [(i, i ^ 1) for i in range(n)])
    return near, far


def body(
    states, inv_sqrt_mass, element_blocks, element_nodes, element_counts, node_counts, boundary_rows
):
    position = lax.axis_index("mesh").astype(jnp.int32).reshape(1)
    devices = lax.axis_size("mesh")
    row_total, width = states.shape
    shared = boundary_rows.shape[2]
    size = element_blocks.shape[1]
    rows = 2 * boundary_rows.reshape(-1)
    nodes = 2 * element_nodes.reshape(-1)
    tall = ((2 * row_total, LANES), F32)
    send = ((2 * shared, LANES), F32)
    mass_rows = inv_sqrt_mass.reshape(-1, LANES)

    stage, values = call(
        "start",
        start_kernel,
        [(position, SMEM), (rows, SMEM), (inv_sqrt_mass, SMEM), (states, HBM)],
        [(tall, KEPT), (((2 * shared + 8, LANES), F32), VMEM)],
        scratch=[pltpu.VMEM((shared, LANES), F32), pltpu.SemaphoreType.DMA((2,))],
        mib=2,
    )
    owner = passed_along(values, "mesh", 1)
    w0, m, *accs = call(
        "convert",
        convert_kernel,
        [(mass_rows, VMEM), (stage, KEPT)],
        [(tall, KEPT)] * (2 + ACCS),
        aliases={1: 1 + ACCS},
        mib=2,
        flops=10 * row_total * width,
    )

    def ham(stage, received, w, m, accs):
        ins = [(element_counts, SMEM), (position, SMEM), (nodes, SMEM), (rows, SMEM)]
        ins += [(r, VMEM) for r in received]
        first = len(ins)
        ins += [(v, KEPT) for v in (w, m, *accs)] + [(element_blocks, HBM)]
        w, m, *accs, near, far = call(
            "ham%d" % stage,
            functools.partial(ham_kernel, stage),
            ins,
            [(tall, KEPT)] * (2 + ACCS) + [(send, VMEM)] * 2,
            aliases={first + i: i for i in range(2 + ACCS)},
            scratch=[
                pltpu.VMEM((2 * size, LANES), F32),
                pltpu.VMEM((size, width), jnp.bfloat16),
                pltpu.VMEM((2 * size, LANES), F32),
                pltpu.VMEM((2 * size, LANES), F32),
                pltpu.VMEM((shared, LANES), F32),
                pltpu.VMEM(element_blocks.shape[1:], element_blocks.dtype),
                pltpu.VMEM(element_blocks.shape[1:], element_blocks.dtype),
                pltpu.SemaphoreType.DMA((2,)),
            ],
            mib=4,
        )
        return w, m, accs, near, far

    def combine(stage, w, m, old, accs):
        ins = [(w, KEPT), (m, KEPT)] + ([(old, KEPT)] if stage > 1 else [])
        first = len(ins)
        ins += [(acc, KEPT) for acc in accs]
        aliases = {first + i: 1 + i for i in range(ACCS * (stage < 3))}
        if stage > 1:
            aliases[2] = 0
        new, *accs = call(
            "combine%d" % stage,
            functools.partial(combine_kernel, stage),
            ins,
            [(tall, KEPT)] * (1 + ACCS * (stage < 3)),
            aliases=aliases,
            mib=1,
            flops=10 * row_total * width,
        )
        return new, accs

    w0, m, accs, near, far = ham(1, [owner], w0, m, accs)
    received = exchanged(near, far)
    w1, accs = combine(1, w0, m, None, accs)
    w1, m, accs, near, far = ham(2, received, w1, m, accs)
    received = exchanged(near, far)
    w2, accs = combine(2, w1, m, w0, accs)
    w2, m, accs, near, far = ham(3, received, w2, m, accs)
    received = exchanged(near, far)
    f, accs = combine(3, w2, m, w1, accs)
    wide = ((width, 2 * width), F32)
    pool = ((4 * shared, LANES), F32)
    f, saved, gram = call(
        "inner",
        inner_kernel,
        [(node_counts, SMEM), (position, SMEM), (rows, SMEM), (f, KEPT)],
        [(tall, KEPT), (pool, KEPT), (wide, KEPT)],
        aliases={3: 0},
        mib=4,
        flops=10 * row_total * width,
    )
    half = ((LANES + 8, LANES), F32)
    f, keep, give = call(
        "finish",
        finish_kernel,
        [(position, SMEM), (rows, SMEM), (received[0], VMEM), (received[1], VMEM)]
        + [(m, KEPT), (saved, KEPT), (gram, KEPT), (f, KEPT)],
        [(tall, KEPT), (half, VMEM), (half, VMEM)],
        aliases={7: 0},
        scratch=[pltpu.VMEM(*pool), pltpu.VMEM(*wide)],
        mib=4,
    )
    mine, other = sum_over_devices(keep, give)
    (rotated,) = call(
        "rotate",
        functools.partial(rotate_kernel, total_of=lambda t: t - shared * (devices - 1)),
        [(node_counts, SMEM), (position, SMEM), (mine, VMEM), (other, VMEM), (f, KEPT)],
        [((states.shape, F32), HBM)],
        scratch=[
            pltpu.VMEM(states.shape, F32),
            pltpu.VMEM((LANES, LANES), F32),
            pltpu.VMEM((3, LANES, LANES), F32),
            pltpu.VMEM((2 * width, width), jnp.bfloat16),
            pltpu.SemaphoreType.DMA((1,)),
        ],
        mib=24,
    )
    return rotated


def solution(mesh):
    in_specs = (
        P("mesh", None),
        P("mesh"),
        P("mesh", None, None),
        P("mesh", None),
        P("mesh"),
        P(),
        P("mesh", None, None),
    )
    out_specs = P("mesh", None)
    return jax.shard_map(body, mesh=mesh, in_specs=in_specs, out_specs=out_specs, check_vma=False)
```

```python
import functools

import jax
import jax.numpy as jnp
from jax import lax
from jax.experimental import pallas as pl
from jax.experimental.pallas import tpu as pltpu
from jax.sharding import PartitionSpec as P

CENTER = 0.5
HALF_WIDTH = 1.5
LANES = 128
ACCS = 4
UNROLL = 256
F32 = jnp.float32
SMEM = pl.BlockSpec(memory_space=pltpu.SMEM)
VMEM = pl.BlockSpec(memory_space=pltpu.VMEM)
HBM = pl.BlockSpec(memory_space=pl.ANY)
KEPT = object()


def passed_along(block, axis, distance):
    devices = range(lax.axis_size(axis))
    route = [(i - distance, i) for i in devices if i - distance in devices]
    return lax.ppermute(block, axis, route)


def pair(offset):
    return pl.ds(pl.multiple_of(offset, 2), 2)


def span(start, size):
    return pl.ds(pl.multiple_of(start, size), size)


def call(name, kernel, ins, outs, aliases=None, scratch=(), mib=8, flops=0):
    operands, in_specs = [], []
    for value, spec in ins:
        if spec is KEPT:
            value = pltpu.with_memory_space_constraint(value, pltpu.VMEM)
        elif spec is HBM:
            value = pltpu.with_memory_space_constraint(value, pltpu.HBM)
        operands.append(value)
        in_specs.append(VMEM if spec is KEPT else spec)
    return pl.pallas_call(
        kernel,
        out_shape=[
            pltpu.VMEM(shape, dtype) if spec is KEPT else jax.ShapeDtypeStruct(shape, dtype)
            for (shape, dtype), spec in outs
        ],
        in_specs=in_specs,
        out_specs=[VMEM if spec is KEPT else spec for _, spec in outs],
        input_output_aliases=aliases or {},
        scratch_shapes=list(scratch),
        compiler_params=pltpu.CompilerParams(vmem_limit_bytes=mib * 2**20),
        cost_estimate=pl.CostEstimate(flops=flops, bytes_accessed=flops, transcendentals=0),
        name=name,
    )(*operands)


def start_kernel(position, rows, mass, states_hbm, stage, send, lines, sems):
    shared = lines.shape[0]
    total = mass.shape[0]
    loads = [
        pltpu.make_async_copy(
            states_hbm.at[:, h * LANES : (h + 1) * LANES],
            stage.at[h * total : (h + 1) * total, :],
            sems.at[h],
        )
        for h in range(2)
    ]
    for load in loads:
        load.start()
    unroll = 32

    def spread(g, carry):
        some = rows.at[pl.ds(shared + g * unroll, unroll)]
        for k in range(unroll):
            lines[pl.ds(g * unroll + k, 1), :] = jnp.full((1, LANES), mass[some[k] >> 1], F32)
        return carry

    lax.fori_loop(0, shared // unroll, spread, 0)
    diagonal = lax.broadcasted_iota(jnp.int32, (LANES, LANES), 0) == lax.broadcasted_iota(
        jnp.int32, (LANES, LANES), 1
    )
    send[2 * shared : 2 * shared + 8, :] = jnp.zeros((8, LANES), F32)
    for i in range(shared // LANES):
        block = lines[i * LANES : (i + 1) * LANES, :]
        line = jnp.sum(jnp.where(diagonal, block, 0.0), axis=0, keepdims=True)
        send[2 * shared + i : 2 * shared + i + 1, :] = line
    for load in loads:
        load.wait()

    def pick(g, carry):
        some = rows.at[pl.ds(shared + g * unroll, unroll)]
        first = pl.multiple_of(g * unroll, unroll)
        for k in range(unroll):
            row = some[k] >> 1
            line = lines[pl.ds(first + k, 1), :]
            for h in range(2):
                value = stage[pl.ds(h * total + row, 1), :]
                send[pl.ds(2 * first + 2 * k + h, 1), :] = line * value
        return carry

    lax.fori_loop(0, shared // unroll, pick, 0)


def convert_kernel(mass_all, stage, w, m, *accs):
    count = mass_all.shape[0]
    total = count * LANES

    def convert(i, carry):
        mass = jnp.broadcast_to(mass_all[pl.ds(i, 1), :], (LANES, LANES)).T
        base = 2 * LANES * i
        for h in range(2):
            m[pl.ds(base + h, LANES, stride=2), :] = mass
            w[pl.ds(base + h, LANES, stride=2), :] = mass * stage[span(h * total + LANES * i, LANES), :]
        for acc in accs[:-1]:
            acc[span(base, 2 * LANES), :] = jnp.zeros((2 * LANES, LANES), F32)
        return carry

    lax.fori_loop(0, count, convert, 0)

    def clear(i, carry):
        accs[-1][span(2 * LANES * i, 2 * LANES), :] = jnp.zeros((2 * LANES, LANES), F32)
        return carry

    lax.fori_loop(0, count, clear, 0)


def take_rows(out, rows, base, *sources):
    group = 32

    def step(g, carry):
        some = rows.at[pl.ds(base + g * group, group)]
        first = pl.multiple_of(2 * g * group, 2 * group)
        for k in range(group):
            at = pair(some[k])
            total = sources[0][at, :]
            for source in sources[1:]:
                total = total + source[at, :]
            out[pl.ds(first + 2 * k, 2), :] = total
        return carry

    lax.fori_loop(0, out.shape[0] // (2 * group), step, 0)


def add_rows(target, rows, base, source, m, scale):
    group = 16

    def step(g, carry):
        some = rows.at[pl.ds(base + g * group, group)]
        first = pl.multiple_of(2 * g * group, 2 * group)
        at = [pair(some[k]) for k in range(group)]
        new = []
        for k in range(group):
            mass = m[at[k], :]
            new.append(target[at[k], :] + scale * (mass * mass) * source[pl.ds(first + 2 * k, 2), :])
        for k in range(group):
            target[at[k], :] = new[k]
        return carry

    lax.fori_loop(0, source.shape[0] // (2 * group), step, 0)


def near_base(position, shared):
    return jnp.where(position % 2 == 0, shared, 0)


def ham_kernel(stage, *refs):
    count, position, nodes, rows = refs[:4]
    received = refs[4]
    refs = refs[5:]
    n_field = 2 + ACCS
    blocks_hbm = refs[n_field]
    refs = refs[n_field + 1 :]
    w, m, *accs = refs[:n_field]
    send_near, send_far, picked, x, *parts_pair, lines, block_a, block_b, sems = refs[n_field:]
    block_pair = (block_a, block_b)

    shared = send_far.shape[0] // 2
    size = picked.shape[0] // 2
    live = count[0]
    near = near_base(position[0], shared)
    far = shared - near

    def load(e, parity):
        return pltpu.make_async_copy(blocks_hbm.at[e], block_pair[parity], sems.at[parity])

    load(0, 0).start()

    @pl.when(live > 1)
    def _():
        load(1, 1).start()

    if stage == 1:
        owner = received

        @pl.when(position[0] > 0)
        def _():
            for i in range(shared // LANES):
                line = owner[2 * shared + i : 2 * shared + i + 1, :]
                lines[i * LANES : (i + 1) * LANES, :] = jnp.broadcast_to(line, (LANES, LANES)).T
            unroll = 16

            def patch(g, carry):
                some = rows.at[pl.ds(g * unroll, unroll)]
                first = pl.multiple_of(g * unroll, unroll)
                for k in range(unroll):
                    at = pair(some[k])
                    w[at, :] = owner[pl.ds(2 * first + 2 * k, 2), :]
                    m[at, :] = jnp.broadcast_to(lines[pl.ds(first + k, 1), :], (2, LANES))
                return carry

            lax.fori_loop(0, shared // unroll, patch, 0)
    else:
        add_rows(w, rows, far, received, m, (1.0 if stage == 2 else 2.0) / HALF_WIDTH)

    def convert():
        for h in range(2):
            x[:, h * LANES : (h + 1) * LANES] = picked[pl.ds(h, size, stride=2), :].astype(x.dtype)

    def product(parity, g):
        part = jnp.dot(
            block_pair[parity][span(g * UNROLL, UNROLL), :], x[...], preferred_element_type=F32
        )
        for h in range(2):
            at = pl.ds(2 * UNROLL * g + h, UNROLL, stride=2)
            parts_pair[parity][at, :] = part[:, h * LANES : (h + 1) * LANES]

    take_rows(picked, nodes, 0, w)
    convert()
    load(0, 0).wait()

    def first_product(g, carry):
        product(0, g)
        return carry

    lax.fori_loop(0, size // UNROLL, first_product, 0)
    take_rows(picked, nodes, jnp.minimum(1, live - 1) * size, w)
    convert()

    def element(e, parity):
        other = 1 - parity
        last = live - 1

        @pl.when(e + 2 < live)
        def _():
            load(e + 2, parity).start()

        @pl.when(e + 1 < live)
        def _():
            load(e + 1, other).wait()

        def move(g, inner):
            product(other, g)
            here = nodes.at[pl.ds(e * size + g * UNROLL, UNROLL)]
            ahead = nodes.at[pl.ds(jnp.minimum(e + 2, last) * size + g * UNROLL, UNROLL)]
            first = pl.multiple_of(2 * g * UNROLL, 2 * UNROLL)
            for k in range(UNROLL):
                line = pl.ds(first + 2 * k, 2)
                picked[line, :] = w[pair(ahead[k]), :]
                at = pair(here[k])
                acc = accs[k % ACCS]
                acc[at, :] = acc[at, :] + parts_pair[parity][line, :]
            return inner

        lax.fori_loop(0, size // UNROLL, move, 0)
        convert()

    def two(t, carry):
        element(2 * t, 0)

        @pl.when(2 * t + 1 < live)
        def _():
            element(2 * t + 1, 1)

        return carry

    lax.fori_loop(0, pl.cdiv(live, 2), two, 0)
    take_rows(send_near, rows, near, *accs)
    take_rows(send_far, rows, far, *accs)


def patch_kernel(scale, position, rows, received, m, w_in, w):
    add_rows(w, rows, near_base(position[0], received.shape[0] // 2), received, m, scale)


def combine_kernel(stage, *refs):
    n = 2 + ACCS + (stage > 1)
    w, m = refs[:2]
    accs = refs[n - ACCS : n]
    old = refs[2] if stage > 1 else None
    new, *emptied = refs[n:]
    factor = 1.0 if stage == 1 else 2.0
    scale_h = factor / HALF_WIDTH
    scale_w = -factor * CENTER / HALF_WIDTH
    chunk = 64

    def step(c, carry):
        at = span(c * chunk, chunk)
        total = accs[0][at, :]
        for acc in accs[1:]:
            total = total + acc[at, :]
        mass = m[at, :]
        rest = scale_w * w[at, :]
        if stage > 1:
            rest = rest - old[at, :]
        if stage < 3:
            new[at, :] = scale_h * (mass * mass) * total + rest
        else:
            new[at, :] = scale_h * mass * total + rest / mass
        for acc in emptied:
            acc[at, :] = jnp.zeros((chunk, LANES), F32)
        return carry

    lax.fori_loop(0, w.shape[0] // chunk, step, 0)


def high_low(x):
    high = x.astype(jnp.bfloat16)
    return high, (x - high.astype(F32)).astype(jnp.bfloat16)


def halves(ref, start, size):
    return jnp.concatenate([ref[pl.ds(start + h, size, stride=2), :] for h in range(2)], axis=1)


def add_square(gram, value, size):
    high, low = high_low(value)
    gram[...] += lax.dot_general(
        high,
        jnp.concatenate([high, low], axis=1),
        (((0,), (0,)), ((), ())),
        preferred_element_type=F32,
    )


def inner_kernel(counts, position, rows, f_in, f, saved, gram):
    shared = saved.shape[0] // 4
    take_rows(saved, rows, 0, f)
    unroll = 32

    def blank(g, carry):
        some = rows.at[pl.ds(g * unroll, unroll)]
        for k in range(unroll):
            f[pair(some[k]), :] = jnp.zeros((2, LANES), F32)
        return carry

    lax.fori_loop(0, 2 * shared // unroll, blank, 0)
    gram[...] = jnp.zeros_like(gram)
    limit = counts[position[0]]
    n = 512

    def add_chunk(c, carry):
        live = c * n + lax.broadcasted_iota(jnp.int32, (n, 2 * LANES), 0) < limit
        add_square(gram, jnp.where(live, halves(f, 2 * n * c, n), 0.0), n)
        return carry

    lax.fori_loop(0, pl.cdiv(limit, n), add_chunk, 0)


def finish_kernel(
    position, rows, near_in, far_in, m, saved_in, gram_in, f_in, f, keep, give, saved, gram
):
    shared = near_in.shape[0] // 2
    width = 2 * LANES
    near = near_base(position[0], shared)
    far = shared - near
    scale = 2.0 / HALF_WIDTH
    group = 16

    def step(g, carry):
        for base, source in ((near, near_in), (far, far_in)):
            some = rows.at[pl.ds(base + g * group, group)]
            first = pl.multiple_of(2 * g * group, 2 * group)
            for k in range(group):
                at = pair(some[k])
                line = pair(2 * base + first + 2 * k)
                value = saved_in[line, :] + scale * m[at, :] * source[pl.ds(first + 2 * k, 2), :]
                saved[line, :] = value
                f[at, :] = value
        return carry

    lax.fori_loop(0, shared // group, step, 0)
    gram[...] = gram_in[...]
    add_square(gram, halves(saved, 2 * shared, shared), shared)

    @pl.when(position[0] == 0)
    def _():
        add_square(gram, halves(saved, 0, shared), shared)

    cross = gram[:, width:]
    full = gram[:, :width] + (cross + cross.T)
    row = lax.broadcasted_iota(jnp.int32, (LANES, LANES), 0)
    lane = lax.broadcasted_iota(jnp.int32, (LANES, LANES), 1)
    last = full[LANES:, LANES:]
    both = jnp.where(row >= lane, full[:LANES, :LANES], last)
    diagonal = jnp.sum(jnp.where(row == lane, last, 0.0), axis=0, keepdims=True)
    pieces = (
        (both, jnp.broadcast_to(diagonal, (8, LANES))),
        (full[:LANES, LANES:], jnp.zeros((8, LANES), F32)),
    )
    for core in range(2):

        @pl.when(position[0] % 2 == core)
        def _():
            for out, (block, tail) in ((keep, pieces[core]), (give, pieces[1 - core])):
                out[0:LANES, :] = block
                out[LANES : LANES + 8, :] = tail


def shifted(value, stride, radix, by):
    route = []
    for i in range(lax.axis_size("mesh")):
        digit = i // stride % radix
        route.append((i, i + ((digit + by) % radix - digit) * stride))
    return lax.ppermute(value, "mesh", route)


def add_kernel(*refs):
    total = refs[0][...]
    for ref in refs[1:-1]:
        total = total + ref[...]
    refs[-1][...] = total


def added(*values):
    ins = [(value, VMEM) for value in values]
    return call("add", add_kernel, ins, [((values[0].shape, F32), VMEM)], mib=1)[0]


def sum_over_devices(keep, give):
    total = added(keep, shifted(give, 1, 2, 1))
    stride, devices = 2, lax.axis_size("mesh")
    while stride < devices:
        radix = min(4, devices // stride)
        got = [shifted(total, stride, radix, by) for by in range(1, radix)]
        total = added(total, *got)
        stride *= radix
    return total, shifted(total, 1, 2, 1)


def eliminate(block):
    n = block.shape[0]
    b = 8
    lane = lax.broadcasted_iota(jnp.int32, (b, n), 1)
    sub = lax.broadcasted_iota(jnp.int32, (b, n), 0)

    def line(value, s):
        return jnp.broadcast_to(value[s : s + 1, :], (b, n))

    def columns(value, first):
        return [jnp.broadcast_to(value[:, first + c : first + c + 1], (b, n)) for c in range(b)]

    parts = [block[b * i : b * i + b, :] for i in range(n // b)]
    for q in range(n // b):
        first = b * q
        inside = (lane >= first) & (lane < first + b)
        cols = columns(parts[q], first)
        corner = [[line(cols[c], s) for c in range(s + 1)] for s in range(b)]
        own = jnp.where(inside, jnp.where(lane - first == sub, 1.0, 0.0), parts[q])
        rows = [line(own, s) for s in range(b)]
        recs, low = [], [[None] * b for _ in range(b)]
        for c in range(b):
            recs.append(1.0 / corner[c][c])
            for s in range(c + 1, b):
                low[s][c] = corner[s][c] * recs[c]
            for s in range(c + 1, b):
                for t in range(c + 1, s + 1):
                    corner[s][t] = corner[s][t] - low[s][c] * corner[t][c]
                rows[s] = rows[s] - low[s][c] * rows[c]
        done = jnp.zeros((b, n), F32)
        for s in range(b):
            done = jnp.where(sub == s, rows[s] * lax.rsqrt(corner[s][s]), done)
        solved = [rows[s] * recs[s] for s in range(b)]
        for s in reversed(range(b)):
            for c in range(s):
                solved[c] = solved[c] - low[s][c] * solved[s]
        for i in range(q + 1, n // b):
            cols = columns(parts[i], first)
            terms = [cols[c] * solved[c] for c in range(b)]
            while len(terms) > 1:
                terms = [terms[k] + terms[k + 1] for k in range(0, len(terms), 2)]
            parts[i] = jnp.where(inside, 0.0, parts[i]) - terms[0]
        parts[q] = jnp.where(lane < first + b, done, 0.0)
    return jnp.concatenate(parts, axis=0)


def dot32(a, b, ca, cb):
    return lax.dot_general(
        a,
        b,
        (((ca,), (cb,)), ((), ())),
        precision=lax.Precision.HIGHEST,
        preferred_element_type=F32,
    )


def rotate_kernel(
    counts, position, mine, other, w, out_hbm, out, block, factors, basis, sems, *, total_of
):
    total = lax.fori_loop(0, counts.shape[0], lambda i, t: t + counts[i], jnp.int32(0))
    scale = 1.0 / (jnp.full((LANES, LANES), total_of(total), jnp.int32).astype(F32))
    core = jnp.full((LANES + 8, LANES), position[0] % 2, jnp.int32)
    first = jnp.where(core == 0, mine[...], other[...])
    second = jnp.where(core == 0, other[...], mine[...])
    row = lax.broadcasted_iota(jnp.int32, (LANES, LANES), 0)
    lane = lax.broadcasted_iota(jnp.int32, (LANES, LANES), 1)
    both = first[:LANES, :]
    turned = both.T
    block[...] = jnp.where(row >= lane, both, turned) * scale
    right = second[:LANES, :] * scale
    last = jnp.where(row < lane, both, turned)
    last = jnp.where(row == lane, jnp.broadcast_to(first[LANES : LANES + 1, :], (LANES, LANES)), last)
    factors[2] = last * scale

    def panel(p, carry):
        factors[p] = eliminate(block[...])

        @pl.when(p == 0)
        def _():
            side = dot32(factors[0], right, 1, 0)
            block[...] = factors[2] - dot32(side, side, 0, 0)
            factors[2] = side

        return carry

    lax.fori_loop(0, 2, panel, 0)
    n = 2 * LANES
    top = factors[0].T
    low_right = factors[1].T
    corner = -dot32(top, dot32(factors[2], low_right, 1, 0), 1, 0)
    inverse_t = jnp.concatenate(
        [
            jnp.concatenate([top, corner], axis=1),
            jnp.concatenate([jnp.zeros((LANES, LANES), F32), low_right], axis=1),
        ],
        axis=0,
    )
    basis[0:n, :], basis[n : 2 * n, :] = high_low(inverse_t)
    limit = counts[position[0]]
    size = 512

    def chunk(c, carry):
        at = span(c * size, size)
        high, low = high_low(halves(w, 2 * size * c, size))
        value = jnp.dot(high, basis[0:n, :], preferred_element_type=F32)
        value += jnp.dot(high, basis[n : 2 * n, :], preferred_element_type=F32)
        value += jnp.dot(low, basis[0:n, :], preferred_element_type=F32)
        live = c * size + lax.broadcasted_iota(jnp.int32, (size, n), 0) < limit
        out[at, :] = jnp.where(live, value, 0.0)
        pltpu.make_async_copy(out.at[at, :], out_hbm.at[at, :], sems.at[0]).start()
        return carry

    lax.fori_loop(0, out.shape[0] // size, chunk, 0)
    pltpu.make_async_copy(out, out_hbm, sems.at[0]).wait()


def far_swapped(value):
    n = lax.axis_size("mesh")
    return lax.ppermute(value, "mesh", [(i, i - 1 + 2 * (i % 2)) for i in range(1, n - 1)])


def near_swapped(value):
    return lax.ppermute(value, "mesh", [(i, i ^ 1) for i in range(lax.axis_size("mesh"))])


def body(
    states, inv_sqrt_mass, element_blocks, element_nodes, element_counts, node_counts, boundary_rows
):
    position = lax.axis_index("mesh").astype(jnp.int32).reshape(1)
    devices = lax.axis_size("mesh")
    row_total, width = states.shape
    shared = boundary_rows.shape[2]
    size = element_blocks.shape[1]
    rows = 2 * boundary_rows.reshape(-1)
    nodes = 2 * element_nodes.reshape(-1)
    tall = ((2 * row_total, LANES), F32)
    send = ((2 * shared, LANES), F32)
    mass_rows = inv_sqrt_mass.reshape(-1, LANES)

    stage, values = call(
        "start",
        start_kernel,
        [(position, SMEM), (rows, SMEM), (inv_sqrt_mass, SMEM), (states, HBM)],
        [(tall, KEPT), (((2 * shared + 8, LANES), F32), VMEM)],
        scratch=[pltpu.VMEM((shared, LANES), F32), pltpu.SemaphoreType.DMA((2,))],
        mib=2,
    )
    owner = passed_along(values, "mesh", 1)
    w0, m, *accs = call(
        "convert",
        convert_kernel,
        [(mass_rows, VMEM), (stage, KEPT)],
        [(tall, KEPT)] * (2 + ACCS),
        aliases={1: 1 + ACCS},
        mib=2,
        flops=10 * row_total * width,
    )

    def ham(stage, received, w, m, accs):
        ins = [(element_counts, SMEM), (position, SMEM), (nodes, SMEM), (rows, SMEM)]
        ins += [(received, VMEM)]
        first = len(ins)
        ins += [(v, KEPT) for v in (w, m, *accs)] + [(element_blocks, HBM)]
        w, m, *accs, near, far = call(
            "ham%d" % stage,
            functools.partial(ham_kernel, stage),
            ins,
            [(tall, KEPT)] * (2 + ACCS) + [(send, VMEM)] * 2,
            aliases={first + i: i for i in range(2 + ACCS)},
            scratch=[
                pltpu.VMEM((2 * size, LANES), F32),
                pltpu.VMEM((size, width), jnp.bfloat16),
                pltpu.VMEM((2 * size, LANES), F32),
                pltpu.VMEM((2 * size, LANES), F32),
                pltpu.VMEM((shared, LANES), F32),
                pltpu.VMEM(element_blocks.shape[1:], element_blocks.dtype),
                pltpu.VMEM(element_blocks.shape[1:], element_blocks.dtype),
                pltpu.SemaphoreType.DMA((2,)),
            ],
            mib=4,
        )
        far, near = far_swapped(far), near_swapped(near)
        return w, m, accs, near, far

    def patched(stage, w, m, near):
        return call(
            "patch%d" % stage,
            functools.partial(patch_kernel, (1.0 if stage == 1 else 2.0) / HALF_WIDTH),
            [(position, SMEM), (rows, SMEM), (near, VMEM), (m, KEPT), (w, KEPT)],
            [(tall, KEPT)],
            aliases={4: 0},
            mib=1,
            flops=shared * width,
        )[0]

    def combine(stage, w, m, old, accs):
        ins = [(w, KEPT), (m, KEPT)] + ([(old, KEPT)] if stage > 1 else [])
        first = len(ins)
        ins += [(acc, KEPT) for acc in accs]
        aliases = {first + i: 1 + i for i in range(ACCS * (stage < 3))}
        if stage > 1:
            aliases[2] = 0
        new, *accs = call(
            "combine%d" % stage,
            functools.partial(combine_kernel, stage),
            ins,
            [(tall, KEPT)] * (1 + ACCS * (stage < 3)),
            aliases=aliases,
            mib=1,
            flops=10 * row_total * width,
        )
        return new, accs

    w0, m, accs, near, far = ham(1, owner, w0, m, accs)
    w1, accs = combine(1, w0, m, None, accs)
    w1 = patched(1, w1, m, near)
    w1, m, accs, near, far = ham(2, far, w1, m, accs)
    w2, accs = combine(2, w1, m, w0, accs)
    w2 = patched(2, w2, m, near)
    w2, m, accs, near, far = ham(3, far, w2, m, accs)
    f, accs = combine(3, w2, m, w1, accs)
    wide = ((width, 2 * width), F32)
    pool = ((4 * shared, LANES), F32)
    f, saved, gram = call(
        "inner",
        inner_kernel,
        [(node_counts, SMEM), (position, SMEM), (rows, SMEM), (f, KEPT)],
        [(tall, KEPT), (pool, KEPT), (wide, KEPT)],
        aliases={3: 0},
        mib=4,
        flops=10 * row_total * width,
    )
    half = ((LANES + 8, LANES), F32)
    f, keep, give = call(
        "finish",
        finish_kernel,
        [(position, SMEM), (rows, SMEM), (near, VMEM), (far, VMEM)]
        + [(m, KEPT), (saved, KEPT), (gram, KEPT), (f, KEPT)],
        [(tall, KEPT), (half, VMEM), (half, VMEM)],
        aliases={7: 0},
        scratch=[pltpu.VMEM(*pool), pltpu.VMEM(*wide)],
        mib=4,
    )
    mine, other = sum_over_devices(keep, give)
    (rotated,) = call(
        "rotate",
        functools.partial(rotate_kernel, total_of=lambda t: t - shared * (devices - 1)),
        [(node_counts, SMEM), (position, SMEM), (mine, VMEM), (other, VMEM), (f, KEPT)],
        [((states.shape, F32), HBM)],
        scratch=[
            pltpu.VMEM(states.shape, F32),
            pltpu.VMEM((LANES, LANES), F32),
            pltpu.VMEM((3, LANES, LANES), F32),
            pltpu.VMEM((2 * width, width), jnp.bfloat16),
            pltpu.SemaphoreType.DMA((1,)),
        ],
        mib=24,
    )
    return rotated


def solution(mesh):
    in_specs = (
        P("mesh", None),
        P("mesh"),
        P("mesh", None, None),
        P("mesh", None),
        P("mesh"),
        P(),
        P("mesh", None, None),
    )
    out_specs = P("mesh", None)
    return jax.shard_map(body, mesh=mesh, in_specs=in_specs, out_specs=out_specs, check_vma=False)
```

```python
import functools

import jax
import jax.numpy as jnp
from jax import lax
from jax.experimental import pallas as pl
from jax.experimental.pallas import tpu as pltpu
from jax.sharding import PartitionSpec as P

CENTER = 0.5
HALF_WIDTH = 1.5
LANES = 128
ACCS = 4
UNROLL = 256
F32 = jnp.float32
SMEM = pl.BlockSpec(memory_space=pltpu.SMEM)
VMEM = pl.BlockSpec(memory_space=pltpu.VMEM)
HBM = pl.BlockSpec(memory_space=pl.ANY)
KEPT = object()


def passed_along(block, axis, distance):
    devices = range(lax.axis_size(axis))
    route = [(i - distance, i) for i in devices if i - distance in devices]
    return lax.ppermute(block, axis, route)


def pair(offset):
    return pl.ds(pl.multiple_of(offset, 2), 2)


def span(start, size):
    return pl.ds(pl.multiple_of(start, size), size)


def call(name, kernel, ins, outs, aliases=None, scratch=(), mib=8, flops=0):
    operands, in_specs = [], []
    for value, spec in ins:
        if spec is KEPT:
            value = pltpu.with_memory_space_constraint(value, pltpu.VMEM)
        elif spec is HBM:
            value = pltpu.with_memory_space_constraint(value, pltpu.HBM)
        operands.append(value)
        in_specs.append(VMEM if spec is KEPT else spec)
    return pl.pallas_call(
        kernel,
        out_shape=[
            pltpu.VMEM(shape, dtype) if spec is KEPT else jax.ShapeDtypeStruct(shape, dtype)
            for (shape, dtype), spec in outs
        ],
        in_specs=in_specs,
        out_specs=[VMEM if spec is KEPT else spec for _, spec in outs],
        input_output_aliases=aliases or {},
        scratch_shapes=list(scratch),
        compiler_params=pltpu.CompilerParams(vmem_limit_bytes=mib * 2**20),
        cost_estimate=pl.CostEstimate(flops=flops, bytes_accessed=flops, transcendentals=0),
        name=name,
    )(*operands)


def start_kernel(position, rows, mass, states_hbm, stage, send, lines, sems):
    shared = lines.shape[0]
    total = mass.shape[0]
    loads = [
        pltpu.make_async_copy(
            states_hbm.at[:, h * LANES : (h + 1) * LANES],
            stage.at[h * total : (h + 1) * total, :],
            sems.at[h],
        )
        for h in range(2)
    ]
    for load in loads:
        load.start()
    unroll = 32

    def spread(g, carry):
        some = rows.at[pl.ds(shared + g * unroll, unroll)]
        for k in range(unroll):
            lines[pl.ds(g * unroll + k, 1), :] = jnp.full((1, LANES), mass[some[k] >> 1], F32)
        return carry

    lax.fori_loop(0, shared // unroll, spread, 0)
    diagonal = lax.broadcasted_iota(jnp.int32, (LANES, LANES), 0) == lax.broadcasted_iota(
        jnp.int32, (LANES, LANES), 1
    )
    send[2 * shared : 2 * shared + 8, :] = jnp.zeros((8, LANES), F32)
    for i in range(shared // LANES):
        block = lines[i * LANES : (i + 1) * LANES, :]
        line = jnp.sum(jnp.where(diagonal, block, 0.0), axis=0, keepdims=True)
        send[2 * shared + i : 2 * shared + i + 1, :] = line
    for load in loads:
        load.wait()

    def pick(g, carry):
        some = rows.at[pl.ds(shared + g * unroll, unroll)]
        first = pl.multiple_of(g * unroll, unroll)
        for k in range(unroll):
            row = some[k] >> 1
            line = lines[pl.ds(first + k, 1), :]
            for h in range(2):
                value = stage[pl.ds(h * total + row, 1), :]
                send[pl.ds(2 * first + 2 * k + h, 1), :] = line * value
        return carry

    lax.fori_loop(0, shared // unroll, pick, 0)


def convert_kernel(mass_all, stage, w, m, *accs):
    count = mass_all.shape[0]
    total = count * LANES

    def convert(i, carry):
        mass = jnp.broadcast_to(mass_all[pl.ds(i, 1), :], (LANES, LANES)).T
        base = 2 * LANES * i
        for h in range(2):
            m[pl.ds(base + h, LANES, stride=2), :] = mass
            w[pl.ds(base + h, LANES, stride=2), :] = mass * stage[span(h * total + LANES * i, LANES), :]
        for acc in accs[:-1]:
            acc[span(base, 2 * LANES), :] = jnp.zeros((2 * LANES, LANES), F32)
        return carry

    lax.fori_loop(0, count, convert, 0)

    def clear(i, carry):
        accs[-1][span(2 * LANES * i, 2 * LANES), :] = jnp.zeros((2 * LANES, LANES), F32)
        return carry

    lax.fori_loop(0, count, clear, 0)


def take_rows(out, rows, base, *sources):
    group = 32

    def step(g, carry):
        some = rows.at[pl.ds(base + g * group, group)]
        first = pl.multiple_of(2 * g * group, 2 * group)
        for k in range(group):
            at = pair(some[k])
            total = sources[0][at, :]
            for source in sources[1:]:
                total = total + source[at, :]
            out[pl.ds(first + 2 * k, 2), :] = total
        return carry

    lax.fori_loop(0, out.shape[0] // (2 * group), step, 0)


def add_rows(target, rows, base, source, m, scale):
    group = 16

    def step(g, carry):
        some = rows.at[pl.ds(base + g * group, group)]
        first = pl.multiple_of(2 * g * group, 2 * group)
        at = [pair(some[k]) for k in range(group)]
        new = []
        for k in range(group):
            mass = m[at[k], :]
            new.append(target[at[k], :] + scale * (mass * mass) * source[pl.ds(first + 2 * k, 2), :])
        for k in range(group):
            target[at[k], :] = new[k]
        return carry

    lax.fori_loop(0, source.shape[0] // (2 * group), step, 0)


def near_base(position, shared):
    return jnp.where(position % 2 == 0, shared, 0)


def ham_kernel(stage, *refs):
    count, position, nodes, rows = refs[:4]
    received = refs[4]
    refs = refs[5:]
    n_field = 2 + ACCS
    blocks_hbm = refs[n_field]
    refs = refs[n_field + 1 :]
    w, m, *accs = refs[:n_field]
    send_near, send_far, picked, x, *parts_pair, lines, block_a, block_b, sems = refs[n_field:]
    block_pair = (block_a, block_b)

    shared = send_far.shape[0] // 2
    size = picked.shape[0] // 2
    live = count[0]
    near = near_base(position[0], shared)
    far = shared - near

    def load(e, parity):
        return pltpu.make_async_copy(blocks_hbm.at[e], block_pair[parity], sems.at[parity])

    load(0, 0).start()

    @pl.when(live > 1)
    def _():
        load(1, 1).start()

    if stage == 1:
        owner = received

        @pl.when(position[0] > 0)
        def _():
            for i in range(shared // LANES):
                line = owner[2 * shared + i : 2 * shared + i + 1, :]
                lines[i * LANES : (i + 1) * LANES, :] = jnp.broadcast_to(line, (LANES, LANES)).T
            unroll = 16

            def patch(g, carry):
                some = rows.at[pl.ds(g * unroll, unroll)]
                first = pl.multiple_of(g * unroll, unroll)
                for k in range(unroll):
                    at = pair(some[k])
                    w[at, :] = owner[pl.ds(2 * first + 2 * k, 2), :]
                    m[at, :] = jnp.broadcast_to(lines[pl.ds(first + k, 1), :], (2, LANES))
                return carry

            lax.fori_loop(0, shared // unroll, patch, 0)
    else:
        add_rows(w, rows, far, received, m, (1.0 if stage == 2 else 2.0) / HALF_WIDTH)

    def convert():
        for h in range(2):
            x[:, h * LANES : (h + 1) * LANES] = picked[pl.ds(h, size, stride=2), :].astype(x.dtype)

    def product(parity, g):
        part = jnp.dot(
            block_pair[parity][span(g * UNROLL, UNROLL), :], x[...], preferred_element_type=F32
        )
        for h in range(2):
            at = pl.ds(2 * UNROLL * g + h, UNROLL, stride=2)
            parts_pair[parity][at, :] = part[:, h * LANES : (h + 1) * LANES]

    take_rows(picked, nodes, 0, w)
    convert()
    load(0, 0).wait()

    def first_product(g, carry):
        product(0, g)
        return carry

    lax.fori_loop(0, size // UNROLL, first_product, 0)
    take_rows(picked, nodes, jnp.minimum(1, live - 1) * size, w)
    convert()

    def element(e, parity):
        other = 1 - parity
        last = live - 1

        @pl.when(e + 2 < live)
        def _():
            load(e + 2, parity).start()

        @pl.when(e + 1 < live)
        def _():
            load(e + 1, other).wait()

        def move(g, inner):
            product(other, g)
            here = nodes.at[pl.ds(e * size + g * UNROLL, UNROLL)]
            ahead = nodes.at[pl.ds(jnp.minimum(e + 2, last) * size + g * UNROLL, UNROLL)]
            first = pl.multiple_of(2 * g * UNROLL, 2 * UNROLL)
            for k in range(UNROLL):
                line = pl.ds(first + 2 * k, 2)
                picked[line, :] = w[pair(ahead[k]), :]
                at = pair(here[k])
                acc = accs[k % ACCS]
                acc[at, :] = acc[at, :] + parts_pair[parity][line, :]
            return inner

        lax.fori_loop(0, size // UNROLL, move, 0)
        convert()

    def two(t, carry):
        element(2 * t, 0)

        @pl.when(2 * t + 1 < live)
        def _():
            element(2 * t + 1, 1)

        return carry

    lax.fori_loop(0, pl.cdiv(live, 2), two, 0)
    take_rows(send_near, rows, near, *accs)
    take_rows(send_far, rows, far, *accs)


def patch_kernel(scale, position, rows, received, m, w_in, w):
    add_rows(w, rows, near_base(position[0], received.shape[0] // 2), received, m, scale)


def combine_kernel(stage, *refs):
    n = 2 + ACCS + (stage > 1)
    w, m = refs[:2]
    accs = refs[n - ACCS : n]
    old = refs[2] if stage > 1 else None
    new, *emptied = refs[n:]
    factor = 1.0 if stage == 1 else 2.0
    scale_h = factor / HALF_WIDTH
    scale_w = -factor * CENTER / HALF_WIDTH
    chunk = 64

    def step(c, carry):
        at = span(c * chunk, chunk)
        total = accs[0][at, :]
        for acc in accs[1:]:
            total = total + acc[at, :]
        mass = m[at, :]
        rest = scale_w * w[at, :]
        if stage > 1:
            rest = rest - old[at, :]
        if stage < 3:
            new[at, :] = scale_h * (mass * mass) * total + rest
        else:
            new[at, :] = scale_h * mass * total + rest / mass
        for acc in emptied:
            acc[at, :] = jnp.zeros((chunk, LANES), F32)
        return carry

    lax.fori_loop(0, w.shape[0] // chunk, step, 0)


def high_low(x):
    high = x.astype(jnp.bfloat16)
    return high, (x - high.astype(F32)).astype(jnp.bfloat16)


def halves(ref, start, size):
    return jnp.concatenate([ref[pl.ds(start + h, size, stride=2), :] for h in range(2)], axis=1)


def add_square(gram, value, size):
    high, low = high_low(value)
    gram[...] += lax.dot_general(
        high,
        jnp.concatenate([high, low], axis=1),
        (((0,), (0,)), ((), ())),
        preferred_element_type=F32,
    )


def inner_kernel(counts, position, rows, f_in, f, saved, gram):
    shared = saved.shape[0] // 4
    take_rows(saved, rows, 0, f)
    unroll = 32

    def blank(g, carry):
        some = rows.at[pl.ds(g * unroll, unroll)]
        for k in range(unroll):
            f[pair(some[k]), :] = jnp.zeros((2, LANES), F32)
        return carry

    lax.fori_loop(0, 2 * shared // unroll, blank, 0)
    gram[...] = jnp.zeros_like(gram)
    limit = counts[position[0]]
    n = 1024

    def add_chunk(c, carry):
        live = c * n + lax.broadcasted_iota(jnp.int32, (n, 2 * LANES), 0) < limit
        add_square(gram, jnp.where(live, halves(f, 2 * n * c, n), 0.0), n)
        return carry

    lax.fori_loop(0, pl.cdiv(limit, n), add_chunk, 0)


def finish_kernel(
    position, rows, near_in, far_in, m, saved_in, gram_in, f_in, f, keep, give, saved, gram
):
    shared = near_in.shape[0] // 2
    width = 2 * LANES
    near = near_base(position[0], shared)
    far = shared - near
    scale = 2.0 / HALF_WIDTH
    group = 16

    def step(g, carry):
        for base, source in ((near, near_in), (far, far_in)):
            some = rows.at[pl.ds(base + g * group, group)]
            first = pl.multiple_of(2 * g * group, 2 * group)
            for k in range(group):
                at = pair(some[k])
                line = pair(2 * base + first + 2 * k)
                value = saved_in[line, :] + scale * m[at, :] * source[pl.ds(first + 2 * k, 2), :]
                saved[line, :] = value
                f[at, :] = value
        return carry

    lax.fori_loop(0, shared // group, step, 0)
    gram[...] = gram_in[...]
    add_square(gram, halves(saved, 2 * shared, shared), shared)

    @pl.when(position[0] == 0)
    def _():
        add_square(gram, halves(saved, 0, shared), shared)

    cross = gram[:, width:]
    full = gram[:, :width] + (cross + cross.T)
    row = lax.broadcasted_iota(jnp.int32, (LANES, LANES), 0)
    lane = lax.broadcasted_iota(jnp.int32, (LANES, LANES), 1)
    last = full[LANES:, LANES:]
    both = jnp.where(row >= lane, full[:LANES, :LANES], last)
    diagonal = jnp.sum(jnp.where(row == lane, last, 0.0), axis=0, keepdims=True)
    pieces = (
        (both, jnp.broadcast_to(diagonal, (8, LANES))),
        (full[:LANES, LANES:], jnp.zeros((8, LANES), F32)),
    )
    for core in range(2):

        @pl.when(position[0] % 2 == core)
        def _():
            for out, (block, tail) in ((keep, pieces[core]), (give, pieces[1 - core])):
                out[0:LANES, :] = block
                out[LANES : LANES + 8, :] = tail


def shifted(value, stride, radix, by):
    route = []
    for i in range(lax.axis_size("mesh")):
        digit = i // stride % radix
        route.append((i, i + ((digit + by) % radix - digit) * stride))
    return lax.ppermute(value, "mesh", route)


def add_kernel(*refs):
    total = refs[0][...]
    for ref in refs[1:-1]:
        total = total + ref[...]
    refs[-1][...] = total


def added(*values):
    ins = [(value, VMEM) for value in values]
    return call("add", add_kernel, ins, [((values[0].shape, F32), VMEM)], mib=1)[0]


def sum_over_devices(keep, give):
    total = added(keep, shifted(give, 1, 2, 1))
    stride, devices = 2, lax.axis_size("mesh")
    while stride < devices:
        radix = min(4, devices // stride)
        got = [shifted(total, stride, radix, by) for by in range(1, radix)]
        total = added(total, *got)
        stride *= radix
    return total, shifted(total, 1, 2, 1)


def eliminate(block):
    n = block.shape[0]
    b = 8
    lane = lax.broadcasted_iota(jnp.int32, (b, n), 1)
    sub = lax.broadcasted_iota(jnp.int32, (b, n), 0)

    def line(value, s):
        return jnp.broadcast_to(value[s : s + 1, :], (b, n))

    def columns(value, first):
        return [jnp.broadcast_to(value[:, first + c : first + c + 1], (b, n)) for c in range(b)]

    parts = [block[b * i : b * i + b, :] for i in range(n // b)]
    for q in range(n // b):
        first = b * q
        inside = (lane >= first) & (lane < first + b)
        cols = columns(parts[q], first)
        corner = [[line(cols[c], s) for c in range(s + 1)] for s in range(b)]
        own = jnp.where(inside, jnp.where(lane - first == sub, 1.0, 0.0), parts[q])
        rows = [line(own, s) for s in range(b)]
        recs, low = [], [[None] * b for _ in range(b)]
        for c in range(b):
            recs.append(1.0 / corner[c][c])
            for s in range(c + 1, b):
                low[s][c] = corner[s][c] * recs[c]
            for s in range(c + 1, b):
                for t in range(c + 1, s + 1):
                    corner[s][t] = corner[s][t] - low[s][c] * corner[t][c]
                rows[s] = rows[s] - low[s][c] * rows[c]
        done = jnp.zeros((b, n), F32)
        for s in range(b):
            done = jnp.where(sub == s, rows[s] * lax.rsqrt(corner[s][s]), done)
        solved = [rows[s] * recs[s] for s in range(b)]
        for s in reversed(range(b)):
            for c in range(s):
                solved[c] = solved[c] - low[s][c] * solved[s]
        for i in range(q + 1, n // b):
            cols = columns(parts[i], first)
            terms = [cols[c] * solved[c] for c in range(b)]
            while len(terms) > 1:
                terms = [terms[k] + terms[k + 1] for k in range(0, len(terms), 2)]
            parts[i] = jnp.where(inside, 0.0, parts[i]) - terms[0]
        parts[q] = jnp.where(lane < first + b, done, 0.0)
    return jnp.concatenate(parts, axis=0)


def dot32(a, b, ca, cb):
    return lax.dot_general(
        a,
        b,
        (((ca,), (cb,)), ((), ())),
        precision=lax.Precision.HIGHEST,
        preferred_element_type=F32,
    )


def rotate_kernel(
    counts, position, mine, other, w, out_hbm, out, block, factors, basis, sems, *, total_of
):
    total = lax.fori_loop(0, counts.shape[0], lambda i, t: t + counts[i], jnp.int32(0))
    scale = 1.0 / (jnp.full((LANES, LANES), total_of(total), jnp.int32).astype(F32))
    core = jnp.full((LANES + 8, LANES), position[0] % 2, jnp.int32)
    first = jnp.where(core == 0, mine[...], other[...])
    second = jnp.where(core == 0, other[...], mine[...])
    row = lax.broadcasted_iota(jnp.int32, (LANES, LANES), 0)
    lane = lax.broadcasted_iota(jnp.int32, (LANES, LANES), 1)
    both = first[:LANES, :]
    turned = both.T
    block[...] = jnp.where(row >= lane, both, turned) * scale
    right = second[:LANES, :] * scale
    last = jnp.where(row < lane, both, turned)
    last = jnp.where(row == lane, jnp.broadcast_to(first[LANES : LANES + 1, :], (LANES, LANES)), last)
    factors[2] = last * scale

    def panel(p, carry):
        factors[p] = eliminate(block[...])

        @pl.when(p == 0)
        def _():
            side = dot32(factors[0], right, 1, 0)
            block[...] = factors[2] - dot32(side, side, 0, 0)
            factors[2] = side

        return carry

    lax.fori_loop(0, 2, panel, 0)
    n = 2 * LANES
    top = factors[0].T
    low_right = factors[1].T
    corner = -dot32(top, dot32(factors[2], low_right, 1, 0), 1, 0)
    inverse_t = jnp.concatenate(
        [
            jnp.concatenate([top, corner], axis=1),
            jnp.concatenate([jnp.zeros((LANES, LANES), F32), low_right], axis=1),
        ],
        axis=0,
    )
    basis[0:n, :], basis[n : 2 * n, :] = high_low(inverse_t)
    limit = counts[position[0]]
    size = 1024

    def chunk(c, carry):
        at = span(c * size, size)
        high, low = high_low(halves(w, 2 * size * c, size))
        value = jnp.dot(high, basis[0:n, :], preferred_element_type=F32)
        value += jnp.dot(high, basis[n : 2 * n, :], preferred_element_type=F32)
        value += jnp.dot(low, basis[0:n, :], preferred_element_type=F32)
        live = c * size + lax.broadcasted_iota(jnp.int32, (size, n), 0) < limit
        out[at, :] = jnp.where(live, value, 0.0)
        pltpu.make_async_copy(out.at[at, :], out_hbm.at[at, :], sems.at[0]).start()
        return carry

    lax.fori_loop(0, out.shape[0] // size, chunk, 0)
    pltpu.make_async_copy(out, out_hbm, sems.at[0]).wait()


def far_swapped(value):
    n = lax.axis_size("mesh")
    return lax.ppermute(value, "mesh", [(i, i - 1 + 2 * (i % 2)) for i in range(1, n - 1)])


def near_swapped(value):
    return lax.ppermute(value, "mesh", [(i, i ^ 1) for i in range(lax.axis_size("mesh"))])


def body(
    states, inv_sqrt_mass, element_blocks, element_nodes, element_counts, node_counts, boundary_rows
):
    position = lax.axis_index("mesh").astype(jnp.int32).reshape(1)
    devices = lax.axis_size("mesh")
    row_total, width = states.shape
    shared = boundary_rows.shape[2]
    size = element_blocks.shape[1]
    rows = 2 * boundary_rows.reshape(-1)
    nodes = 2 * element_nodes.reshape(-1)
    tall = ((2 * row_total, LANES), F32)
    send = ((2 * shared, LANES), F32)
    mass_rows = inv_sqrt_mass.reshape(-1, LANES)

    stage, values = call(
        "start",
        start_kernel,
        [(position, SMEM), (rows, SMEM), (inv_sqrt_mass, SMEM), (states, HBM)],
        [(tall, KEPT), (((2 * shared + 8, LANES), F32), VMEM)],
        scratch=[pltpu.VMEM((shared, LANES), F32), pltpu.SemaphoreType.DMA((2,))],
        mib=2,
    )
    owner = passed_along(values, "mesh", 1)
    w0, m, *accs = call(
        "convert",
        convert_kernel,
        [(mass_rows, VMEM), (stage, KEPT)],
        [(tall, KEPT)] * (2 + ACCS),
        aliases={1: 1 + ACCS},
        mib=2,
        flops=10 * row_total * width,
    )

    def ham(stage, received, w, m, accs):
        ins = [(element_counts, SMEM), (position, SMEM), (nodes, SMEM), (rows, SMEM)]
        ins += [(received, VMEM)]
        first = len(ins)
        ins += [(v, KEPT) for v in (w, m, *accs)] + [(element_blocks, HBM)]
        w, m, *accs, near, far = call(
            "ham%d" % stage,
            functools.partial(ham_kernel, stage),
            ins,
            [(tall, KEPT)] * (2 + ACCS) + [(send, VMEM)] * 2,
            aliases={first + i: i for i in range(2 + ACCS)},
            scratch=[
                pltpu.VMEM((2 * size, LANES), F32),
                pltpu.VMEM((size, width), jnp.bfloat16),
                pltpu.VMEM((2 * size, LANES), F32),
                pltpu.VMEM((2 * size, LANES), F32),
                pltpu.VMEM((shared, LANES), F32),
                pltpu.VMEM(element_blocks.shape[1:], element_blocks.dtype),
                pltpu.VMEM(element_blocks.shape[1:], element_blocks.dtype),
                pltpu.SemaphoreType.DMA((2,)),
            ],
            mib=4,
        )
        far, near = far_swapped(far), near_swapped(near)
        return w, m, accs, near, far

    def patched(stage, w, m, near):
        return call(
            "patch%d" % stage,
            functools.partial(patch_kernel, (1.0 if stage == 1 else 2.0) / HALF_WIDTH),
            [(position, SMEM), (rows, SMEM), (near, VMEM), (m, KEPT), (w, KEPT)],
            [(tall, KEPT)],
            aliases={4: 0},
            mib=1,
            flops=shared * width,
        )[0]

    def combine(stage, w, m, old, accs):
        ins = [(w, KEPT), (m, KEPT)] + ([(old, KEPT)] if stage > 1 else [])
        first = len(ins)
        ins += [(acc, KEPT) for acc in accs]
        aliases = {first + i: 1 + i for i in range(ACCS * (stage < 3))}
        if stage > 1:
            aliases[2] = 0
        new, *accs = call(
            "combine%d" % stage,
            functools.partial(combine_kernel, stage),
            ins,
            [(tall, KEPT)] * (1 + ACCS * (stage < 3)),
            aliases=aliases,
            mib=1,
            flops=10 * row_total * width,
        )
        return new, accs

    w0, m, accs, near, far = ham(1, owner, w0, m, accs)
    w1, accs = combine(1, w0, m, None, accs)
    w1 = patched(1, w1, m, near)
    w1, m, accs, near, far = ham(2, far, w1, m, accs)
    w2, accs = combine(2, w1, m, w0, accs)
    w2 = patched(2, w2, m, near)
    w2, m, accs, near, far = ham(3, far, w2, m, accs)
    f, accs = combine(3, w2, m, w1, accs)
    wide = ((width, 2 * width), F32)
    pool = ((4 * shared, LANES), F32)
    f, saved, gram = call(
        "inner",
        inner_kernel,
        [(node_counts, SMEM), (position, SMEM), (rows, SMEM), (f, KEPT)],
        [(tall, KEPT), (pool, KEPT), (wide, KEPT)],
        aliases={3: 0},
        mib=4,
        flops=10 * row_total * width,
    )
    half = ((LANES + 8, LANES), F32)
    f, keep, give = call(
        "finish",
        finish_kernel,
        [(position, SMEM), (rows, SMEM), (near, VMEM), (far, VMEM)]
        + [(m, KEPT), (saved, KEPT), (gram, KEPT), (f, KEPT)],
        [(tall, KEPT), (half, VMEM), (half, VMEM)],
        aliases={7: 0},
        scratch=[pltpu.VMEM(*pool), pltpu.VMEM(*wide)],
        mib=4,
    )
    mine, other = sum_over_devices(keep, give)
    (rotated,) = call(
        "rotate",
        functools.partial(rotate_kernel, total_of=lambda t: t - shared * (devices - 1)),
        [(node_counts, SMEM), (position, SMEM), (mine, VMEM), (other, VMEM), (f, KEPT)],
        [((states.shape, F32), HBM)],
        scratch=[
            pltpu.VMEM(states.shape, F32),
            pltpu.VMEM((LANES, LANES), F32),
            pltpu.VMEM((3, LANES, LANES), F32),
            pltpu.VMEM((2 * width, width), jnp.bfloat16),
            pltpu.SemaphoreType.DMA((1,)),
        ],
        mib=24,
    )
    return rotated


def solution(mesh):
    in_specs = (
        P("mesh", None),
        P("mesh"),
        P("mesh", None, None),
        P("mesh", None),
        P("mesh"),
        P(),
        P("mesh", None, None),
    )
    out_specs = P("mesh", None)
    return jax.shard_map(body, mesh=mesh, in_specs=in_specs, out_specs=out_specs, check_vma=False)
```
